512 devices in a mesh: section: 4 (over y_hi), seq: 16 (over z, core), dp: 8 (over y_lo, x).
Axes of the slice: x: 4, y: 8 (y_hi: 4, y_lo: 2; y = y_hi * 2 + y_lo), z: 8, core: 2. Of those that a mesh axis runs over, the one named last changes fastest.
Arguments:
- queries: bfloat16 [8, 2048, 2560], P('dp', 'seq', 'section'), may hold values from -64 to 64
- keys: bfloat16 [8, 2048, 2560], P('dp', 'seq', 'section'), may hold values from -64 to 64
- values: bfloat16 [8, 2048, 2560], P('dp', 'seq', 'section'), may hold values from -6 to 6
- grad_out: bfloat16 [8, 2048, 2560], P('dp', 'seq', 'section'), may hold values from -6 to 6
- lengths: int32 [8, 4], P('dp'), may hold values from 1 to 1024, 2048 in all within a row
- query_gain: float32 [2560], P('section'), may hold values from 0.1 to 1.9
- key_gain: float32 [2560], P('section'), may hold values from 0.1 to 1.9
Outputs:
- attended: bfloat16 [8, 2048, 2560], P('dp', 'seq', 'section')
- query_grad: bfloat16 [8, 2048, 2560], P('dp', 'seq', 'section')
- key_grad: bfloat16 [8, 2048, 2560], P('dp', 'seq', 'section')
- value_grad: bfloat16 [8, 2048, 2560], P('dp', 'seq', 'section')
- query_gain_grad: float32 [2560], P('section')
- key_gain_grad: float32 [2560], P('section')
The draws below stay inside these ranges and needn't reach their ends.
Inputs may be any that keep to these rules, and one draw needn't show every extreme that they name: Each micro-batch's 4 clip lengths sum to 2048, and the longest is exactly half of 2048.
All inputs are finite; a program needn't handle non-finite values.
Results may differ from the reference program's by a relative error of at most 0.035.
Values may be sent and summed in bfloat16 or wider, within the bound.
No kernel may reach another device: no remote copies, remote signals or barrier semaphores. Data moves between devices by JAX's collectives and lax.ppermute only.
A program may use at most 64 MiB of HBM per device.

```python
import math
import jax
import jax.numpy as jnp
import numpy as np
from jax import lax

HEADS = 20
HEAD_DIM = 128
CLIPS = 4
DATT = 2560
SEQ = 2048
MICRO = 8


def drawn_rows(key, which):
    base = jnp.clip(jax.random.normal(jax.random.fold_in(key, which), (MICRO, SEQ, DATT), jnp.float32), -6.0, 6.0)
    return base.astype(jnp.bfloat16)


def draw_queries(key, part):
    return drawn_rows(key, 1)


def draw_keys(key, part):
    return drawn_rows(key, 2)


def block_scale(own_key, dims, pieces, least, top_value):
    level = 1.0
    for axis_at, shards_of in pieces:
        heights = jax.random.uniform(jax.random.fold_in(jax.random.fold_in(own_key, 6), axis_at), (shards_of,), jnp.float32, least / len(pieces), top_value / len(pieces))
        level = level * jnp.repeat(jnp.exp(heights), dims[axis_at] // shards_of).reshape((-1,) + (1,) * (len(dims) - 1 - axis_at))
    return level


def length_profile(amount, total, bound, slope):
    loads = [(1 << 20) // math.isqrt(rank ** slope) + 1 for rank in range(2, amount + 1)]
    spare, counts = total - bound - (amount - 1), [1] * (amount - 1)
    while spare > 0:
        free = [i for i in range(amount - 1) if counts[i] < bound]
        whole, budget = sum([loads[i] for i in free]), spare
        for i in free:
            more = min(bound - counts[i], max(1, budget * loads[i] // whole), spare)
            counts[i] = counts[i] + more
            spare = spare - more
    return np.array([bound] + counts)


def uneven_parts(stream_key, amount, total, reach, slope):
    if amount == 2:
        one = jax.random.randint(stream_key, (), max(1, total - reach), min(reach, total - 1) + 1)
        return jnp.stack([one, total - one])
    tallies = jnp.asarray(length_profile(amount, total, reach, slope), jnp.int32)
    pairs = (amount - 1) // 2
    donor, receiver = tallies[1:1 + 2 * pairs:2], tallies[2:2 + 2 * pairs:2]
    margin = jnp.minimum(donor - 1, reach - receiver)
    moved = jax.random.randint(jax.random.fold_in(stream_key, 1), (pairs,), 0, 1 << 20) % (margin + 1)
    tallies = tallies.at[1:1 + 2 * pairs:2].set(donor - moved).at[2:2 + 2 * pairs:2].set(receiver + moved)
    return tallies[jax.random.permutation(jax.random.fold_in(stream_key, 2), amount)]


def centred(own_key, shape, spread, limit, pieces=(), held_as=jnp.bfloat16):
    drawn = jax.random.normal(own_key, shape, jnp.float32) * spread
    if len(pieces) > 0:
        drawn = block_scale(own_key, shape, pieces, -0.22, 0.18) * drawn
    return jnp.clip(drawn, min=-limit, max=limit).astype(held_as)


def setup_inputs(seed: int = 0) -> dict:
    key_list = jax.random.split(jax.random.key(seed), 8)
    return {
        "queries": draw_queries(jax.random.fold_in(key_list[7], 71), 0),
        "keys": draw_keys(jax.random.fold_in(key_list[7], 71), 0),
        "values": centred(key_list[2], (MICRO, SEQ, DATT), 1.0, 6.0, ((0, 8), (1, 16), (2, 4))),
        "grad_out": centred(key_list[3], (MICRO, SEQ, DATT), 1.0, 6.0, ((0, 8), (1, 16), (2, 4))),
        "lengths": jax.vmap(lambda own: uneven_parts(own, CLIPS, SEQ, SEQ // 2, 2))(jax.random.split(key_list[4], MICRO)).reshape((MICRO, CLIPS)).astype(jnp.int32),
        "query_gain": jnp.clip(1.0 + 0.18 * jax.random.normal(key_list[5], (DATT,), jnp.float32), 0.1, 1.9),
        "key_gain": jnp.clip(1.0 + 0.18 * jax.random.normal(key_list[6], (DATT,), jnp.float32), 0.1, 1.9),
    }


norm_eps = 1e-06
masked_score = -1e+30

def clip_index(lengths_row, positions):
    ends = jnp.cumsum(lengths_row)
    return lax.optimization_barrier(jnp.sum((positions[:, None] >= ends[None, :]).astype(jnp.int32), axis=1))

def normalize(inputs, gain):
    floats = inputs.astype(jnp.float32)
    squares = lax.optimization_barrier(jnp.sum(floats * floats, axis=-1))
    inverse = lax.rsqrt(squares / DATT + norm_eps)
    return ((floats * inverse[:, None] * gain[None, :]).astype(jnp.bfloat16), inverse)

def norm_back(inputs, inverse, gain, grad_norm):
    floats = inputs.astype(jnp.float32)
    inner = lax.optimization_barrier(jnp.sum(gain[None, :] * grad_norm * floats, axis=-1))
    grad = inverse[:, None] * gain[None, :] * grad_norm - floats * (inverse ** 3)[:, None] * inner[:, None] / DATT
    gain_part = lax.optimization_barrier(jnp.sum(grad_norm * floats * inverse[:, None], axis=0))
    return (grad.astype(jnp.bfloat16), gain_part)

def split_heads(matrix):
    return matrix.reshape(SEQ, HEADS, HEAD_DIM).transpose(1, 0, 2)

def merge_heads(stacked):
    return stacked.transpose(1, 0, 2).reshape(SEQ, DATT)

def reference(queries, keys, values, grad_out, lengths, query_gain, key_gain):
    scale = 1.0 / math.sqrt(HEAD_DIM)

    def one_batch(inputs):
        query_rows, key_rows, value_rows, grad_rows, clip_lengths = inputs
        positions = jnp.arange(SEQ, dtype=jnp.int32)
        clip_ids = clip_index(clip_lengths, positions)
        allowed = clip_ids[:, None] == clip_ids[None, :]
        query_norm, query_inv = normalize(query_rows, query_gain)
        key_norm, key_inv = normalize(key_rows, key_gain)

        def one_head(parts):
            query_head, key_head, value_head, grad_head = parts
            scores = jnp.dot(query_head, key_head.T, preferred_element_type=jnp.float32) * scale
            scores = jnp.where(allowed, scores, masked_score)
            row_max = lax.optimization_barrier(jnp.max(scores, axis=1))
            weights = jnp.where(allowed, jnp.exp(scores - row_max[:, None]), 0.0)
            row_total = lax.optimization_barrier(jnp.sum(weights, axis=1))
            attended = (jnp.dot(weights.astype(jnp.bfloat16), value_head, preferred_element_type=jnp.float32) / row_total[:, None]).astype(jnp.bfloat16)
            log_total = row_max + jnp.log(row_total)
            probs = jnp.where(allowed, jnp.exp(scores - log_total[:, None]), 0.0)
            delta = lax.optimization_barrier(jnp.sum(grad_head.astype(jnp.float32) * attended.astype(jnp.float32), axis=1))
            value_grad = jnp.dot(probs.astype(jnp.bfloat16).T, grad_head, preferred_element_type=jnp.float32)
            grad_probs = jnp.dot(grad_head, value_head.T, preferred_element_type=jnp.float32)
            grad_scores = (probs * (grad_probs - delta[:, None])).astype(jnp.bfloat16)
            query_norm_grad = jnp.dot(grad_scores, key_head, preferred_element_type=jnp.float32) * scale
            key_norm_grad = jnp.dot(grad_scores.T, query_head, preferred_element_type=jnp.float32) * scale
            return (attended, value_grad, query_norm_grad, key_norm_grad)
        attended, value_grad, query_norm_grad, key_norm_grad = lax.map(one_head, (split_heads(query_norm), split_heads(key_norm), split_heads(value_rows), split_heads(grad_rows)))
        query_grad, query_part = norm_back(query_rows, query_inv, query_gain, merge_heads(query_norm_grad))
        key_grad, key_part = norm_back(key_rows, key_inv, key_gain, merge_heads(key_norm_grad))
        return (merge_heads(attended), query_grad, key_grad, merge_heads(value_grad).astype(jnp.bfloat16), query_part, key_part)
    attended, query_grad, key_grad, value_grad, query_parts, key_parts = lax.map(one_batch, (queries, keys, values, grad_out, lengths))
    return (attended, query_grad, key_grad, value_grad, lax.optimization_barrier(jnp.sum(query_parts, axis=0)), lax.optimization_barrier(jnp.sum(key_parts, axis=0)))
```

```python
import functools
import math

import jax
import jax.numpy as jnp
from jax import lax
from jax.experimental import pallas as pl
from jax.experimental.pallas import tpu as pltpu
from jax.sharding import PartitionSpec as P

HEAD_DIM = 128
BLOCK = 128
norm_eps = 1e-06
masked_score = -1e30


def attention_kernel(blocks, extra, info, own_in, other_in, own_out, other_out, win, kacc, vacc):
    span = win.shape[1] // BLOCK
    width = span * BLOCK
    total = blocks * BLOCK
    scale = 1.0 / math.sqrt(HEAD_DIM)
    first = info[0]
    core = info[1]
    long_clip = info[2]

    def place(j):
        block = lax.rem(first + j, blocks)
        return lax.div(block, 2), lax.rem(block, 2) == core

    for j in range(span):
        at, mine = place(j)
        for t in range(4):
            a = own_in[at, t * BLOCK : (t + 1) * BLOCK, :]
            b = other_in[at, t * BLOCK : (t + 1) * BLOCK, :]
            win[t, j * BLOCK : (j + 1) * BLOCK, :] = jnp.where(mine, a, b)

    def clip_of(offset, shape, axis):
        token = lax.rem(first * BLOCK + offset + lax.broadcasted_iota(jnp.int32, shape, axis), total)
        clip = jnp.zeros(shape, jnp.int32)
        for c in range(4):
            clip = clip + (token >= info[3 + c]).astype(jnp.int32)
        valid = (clip == long_clip) == (core == 0)
        return clip, valid

    key_clip, key_valid = clip_of(0, (1, width), 1)
    key_clip = jnp.where(key_valid, key_clip, -1)
    keys = win[1]
    values = win[2]
    rows = 3 * BLOCK
    own_out[...] = jnp.zeros_like(own_out)
    other_out[...] = jnp.zeros_like(other_out)
    query_gain = jnp.zeros((1, HEAD_DIM), jnp.float32)

    def put(j, t, block_value):
        at, mine = place(j)

        @pl.when(mine)
        def _():
            own_out[at, t * BLOCK : (t + 1) * BLOCK, :] = block_value

        @pl.when(jnp.logical_not(mine))
        def _():
            other_out[at, t * BLOCK : (t + 1) * BLOCK, :] = block_value

    nt = (((1,), (1,)), ((), ()))
    tn = (((0,), (0,)), ((), ()))
    for i in range(width // rows):
        query = win[0, i * rows : (i + 1) * rows, :]
        grad = win[3, i * rows : (i + 1) * rows, :]
        row_clip, row_valid = clip_of(i * rows, (rows, 1), 0)
        row_clip = jnp.where(row_valid, row_clip, -2)
        scores = lax.dot_general(query, keys, nt, preferred_element_type=jnp.float32)
        scores = jnp.where(row_clip == key_clip, scores * (scale * math.log2(math.e)), masked_score)
        row_max = jnp.max(scores, axis=1, keepdims=True)
        weights = jnp.exp2(scores - row_max)
        row_total = jnp.sum(weights, axis=1, keepdims=True)
        row_inv = jnp.where(row_valid, 1.0 / row_total, 0.0)
        low = weights.astype(jnp.bfloat16)
        attended = jnp.dot(low, values, preferred_element_type=jnp.float32) * row_inv
        grad_part = (grad.astype(jnp.float32) * row_inv).astype(jnp.bfloat16)
        dots = lax.dot_general(grad_part, values, nt, preferred_element_type=jnp.float32)
        delta = jnp.sum(weights * dots, axis=1, keepdims=True) * row_inv
        grad_scores = (weights * (dots - delta)).astype(jnp.bfloat16)
        query_norm_grad = jnp.dot(grad_scores, keys, preferred_element_type=jnp.float32) * scale
        value_part = lax.dot_general(low, grad_part, tn, preferred_element_type=jnp.float32)
        key_part = lax.dot_general(grad_scores, query, tn, preferred_element_type=jnp.float32)
        if i == 0:
            vacc[...] = value_part
            kacc[...] = key_part
        else:
            vacc[...] += value_part
            kacc[...] += key_part
        query_gain = query_gain + jnp.sum(query_norm_grad * query.astype(jnp.float32), axis=0, keepdims=True)
        attended = attended.astype(jnp.bfloat16)
        query_norm_grad = query_norm_grad.astype(jnp.bfloat16)
        for r in range(rows // BLOCK):
            put(i * (rows // BLOCK) + r, 0, attended[r * BLOCK : (r + 1) * BLOCK])
            put(i * (rows // BLOCK) + r, 1, query_norm_grad[r * BLOCK : (r + 1) * BLOCK])
    key_norm_grad = kacc[...] * scale
    key_gain = jnp.sum(key_norm_grad * keys.astype(jnp.float32), axis=0, keepdims=True)
    key_norm_grad = key_norm_grad.astype(jnp.bfloat16)
    value_grad = vacc[...].astype(jnp.bfloat16)
    for j in range(span):
        put(j, 2, key_norm_grad[j * BLOCK : (j + 1) * BLOCK])
        put(j, 3, value_grad[j * BLOCK : (j + 1) * BLOCK])

    parts = []
    for total_row in (query_gain, key_gain):
        high = total_row.astype(jnp.bfloat16).astype(jnp.float32)
        parts += [high, total_row - high]
    zero = jnp.zeros((4, HEAD_DIM), jnp.float32)
    pad = jnp.zeros((extra - 8, HEAD_DIM), jnp.float32)
    four = jnp.concatenate(parts, axis=0)
    here = jnp.concatenate([four, zero, pad], axis=0).astype(jnp.bfloat16)
    there = jnp.concatenate([zero, four, pad], axis=0).astype(jnp.bfloat16)
    for at in range(blocks // 2):
        own_out[at, 4 * BLOCK :, :] = here
        other_out[at, 4 * BLOCK :, :] = there


def local(queries, keys, values, grad_out, lengths, query_gain, key_gain):
    rows, width = queries.shape[1:]
    heads = width // HEAD_DIM
    total_width = width * lax.axis_size("section")
    seq = lax.axis_size("seq")
    chips = seq // 2
    extra = 16
    chunk = 4 * rows + extra
    index = lax.axis_index("seq")
    core = lax.rem(index, 2)
    same_core = [[2 * z + c for z in range(chips)] for c in range(2)]
    other_core = [(i, i ^ 1) for i in range(seq)]

    query_float = queries[0].astype(jnp.float32)
    key_float = keys[0].astype(jnp.float32)
    squares = jnp.stack([jnp.sum(query_float * query_float, axis=1), jnp.sum(key_float * key_float, axis=1)])
    squares = jnp.sum(lax.all_gather(squares, "section"), axis=0)
    inverse = lax.rsqrt(squares / total_width + norm_eps)
    query_inv, key_inv = inverse[0][:, None], inverse[1][:, None]
    query_norm = (query_float * query_inv * query_gain[None, :]).astype(jnp.bfloat16)
    key_norm = (key_float * key_inv * key_gain[None, :]).astype(jnp.bfloat16)

    def split(matrix):
        return matrix.reshape(rows, heads, HEAD_DIM).transpose(1, 0, 2)

    packed = jnp.stack([split(query_norm), split(key_norm), split(values[0]), split(grad_out[0])], axis=1)
    packed = packed.reshape(heads, 4 * rows, HEAD_DIM)
    packed = jnp.pad(packed, ((0, chips - heads), (0, 0), (0, 0)))
    own = lax.all_to_all(packed, "seq", 0, 0, axis_index_groups=same_core, tiled=True)
    other = lax.ppermute(own, "seq", other_core)

    sizes = lengths[0]
    ends = [sizes[0]]
    for c in range(1, 4):
        ends.append(ends[-1] + sizes[c])
    half = seq * rows // 2
    long_clip = jnp.int32(0)
    begin = jnp.int32(0)
    for c in range(1, 4):
        is_long = sizes[c] == half
        long_clip = jnp.where(is_long, c, long_clip)
        begin = jnp.where(is_long, ends[c - 1], begin)
    first = lax.rem(lax.div(begin, rows) + core * (seq // 2), seq)
    info = jnp.stack([first, core, long_clip, *ends]).astype(jnp.int32)

    window = (seq // 2 + 1) * BLOCK
    out_block = jax.ShapeDtypeStruct((chips, chunk, HEAD_DIM), jnp.bfloat16)
    in_vmem = pl.BlockSpec(memory_space=pltpu.VMEM)
    own_out, other_out = pl.pallas_call(
        functools.partial(attention_kernel, seq, extra),
        out_shape=(out_block, out_block),
        in_specs=[pl.BlockSpec(memory_space=pltpu.SMEM), in_vmem, in_vmem],
        out_specs=(in_vmem, in_vmem),
        scratch_shapes=[
            pltpu.VMEM((4, window, HEAD_DIM), jnp.bfloat16),
            pltpu.VMEM((window, HEAD_DIM), jnp.float32),
            pltpu.VMEM((window, HEAD_DIM), jnp.float32),
        ],
        compiler_params=pltpu.CompilerParams(vmem_limit_bytes=48 * 2**20),
        cost_estimate=pl.CostEstimate(
            flops=12 * window * window * HEAD_DIM,
            transcendentals=window * window,
            bytes_accessed=4 * chips * chunk * HEAD_DIM * 2,
        ),
        name="attention",
    )(info, own, other)

    merged = own_out + lax.ppermute(other_out, "seq", other_core)
    back = lax.all_to_all(merged, "seq", 0, 0, axis_index_groups=same_core, tiled=True)[:heads]

    def take(t):
        return back[:, t * rows : (t + 1) * rows].transpose(1, 0, 2).reshape(rows, width)

    attended, value_grad = take(0), take(3)
    query_flat = take(1).astype(jnp.float32)
    key_flat = take(2).astype(jnp.float32)
    gains = back[:, 4 * rows : 4 * rows + 8].astype(jnp.float32)
    query_sum = (gains[:, 0] + gains[:, 1] + gains[:, 4] + gains[:, 5]).reshape(width)
    key_sum = (gains[:, 2] + gains[:, 3] + gains[:, 6] + gains[:, 7]).reshape(width)
    query_gain_grad, key_gain_grad = lax.psum((query_sum / query_gain, key_sum / key_gain), "dp")

    inner = jnp.stack(
        [
            jnp.sum(query_gain[None, :] * query_flat * query_float, axis=1),
            jnp.sum(key_gain[None, :] * key_flat * key_float, axis=1),
        ]
    )
    inner = jnp.sum(lax.all_gather(inner, "section"), axis=0)
    query_grad = query_inv * query_gain[None, :] * query_flat - query_float * (
        query_inv**3 * inner[0][:, None] / total_width
    )
    key_grad = key_inv * key_gain[None, :] * key_flat - key_float * (
        key_inv**3 * inner[1][:, None] / total_width
    )
    return (
        attended[None],
        query_grad.astype(jnp.bfloat16)[None],
        key_grad.astype(jnp.bfloat16)[None],
        value_grad[None],
        query_gain_grad,
        key_gain_grad,
    )


def solution(mesh):
    rows = P("dp", "seq", "section")
    features = P("section")
    return jax.shard_map(
        local,
        mesh=mesh,
        in_specs=(rows, rows, rows, rows, P("dp", None), features, features),
        out_specs=(rows, rows, rows, rows, features, features),
        check_vma=False,
    )
```

```python
import functools
import math

import jax
import jax.numpy as jnp
from jax import lax
from jax.experimental import pallas as pl
from jax.experimental.pallas import tpu as pltpu
from jax.sharding import PartitionSpec as P

HEAD_DIM = 128
BLOCK = 128
norm_eps = 1e-06
masked_score = -1e30

VMEM = pl.BlockSpec(memory_space=pltpu.VMEM)
SMEM = pl.BlockSpec(memory_space=pltpu.SMEM)


def as_row(column):
    return jnp.broadcast_to(column, (BLOCK, BLOCK)).T[0:1]


def as_column(row):
    return jnp.broadcast_to(row, (BLOCK, BLOCK)).T[:, 0:1]


def squares_kernel(queries, keys, out):
    out[...] = jnp.zeros_like(out)
    for t, ref in enumerate((queries, keys)):
        floats = ref[0].astype(jnp.float32)
        out[t : t + 1, :] = as_row(jnp.sum(floats * floats, axis=1, keepdims=True))


def inverses(squares, total_width):
    summed = jnp.sum(squares[...], axis=0)
    inverse = lax.rsqrt(summed / total_width + norm_eps)
    return as_column(inverse[0:1]), as_column(inverse[1:2])


def pack_plain_kernel(first, second, out):
    heads = first.shape[2] // HEAD_DIM
    for h in range(heads):
        for t, ref in enumerate((first, second)):
            out[h, t * BLOCK : (t + 1) * BLOCK, :] = ref[0, :, h * HEAD_DIM : (h + 1) * HEAD_DIM]
    for h in range(heads, out.shape[0]):
        out[h] = jnp.zeros(out.shape[1:], out.dtype)


def pack_normed_kernel(total_width, queries, keys, squares, query_gain, key_gain, out):
    heads = queries.shape[2] // HEAD_DIM
    invs = inverses(squares, total_width)
    for t, (ref, gain) in enumerate(((queries, query_gain), (keys, key_gain))):
        for h in range(heads):
            cols = slice(h * HEAD_DIM, (h + 1) * HEAD_DIM)
            normed = ref[0, :, cols].astype(jnp.float32) * invs[t] * gain[0:1, cols]
            out[h, t * BLOCK : (t + 1) * BLOCK, :] = normed.astype(jnp.bfloat16)
    for h in range(heads, out.shape[0]):
        out[h] = jnp.zeros(out.shape[1:], out.dtype)


def attention_kernel(
    blocks,
    lengths,
    own_normed,
    other_normed,
    own_plain,
    other_plain,
    own_av,
    other_av,
    own_qk,
    other_qk,
    own_inner,
    other_inner,
    win,
    kacc,
    vacc,
):
    span = win.shape[1] // BLOCK
    width = span * BLOCK
    total = blocks * BLOCK
    scale = 1.0 / math.sqrt(HEAD_DIM)
    core = lax.rem(lax.axis_index("seq"), 2)
    ends = [lengths[0, 0]]
    long_clip = jnp.int32(0)
    begin = jnp.int32(0)
    for c in range(1, 4):
        is_long = lengths[0, c] == total // 2
        long_clip = jnp.where(is_long, c, long_clip)
        begin = jnp.where(is_long, ends[-1], begin)
        ends.append(ends[-1] + lengths[0, c])
    first = lax.rem(lax.div(begin, BLOCK) + core * (blocks // 2), blocks)

    def place(j):
        block = lax.rem(first + j, blocks)
        return lax.div(block, 2), lax.rem(block, 2) == core

    for j in range(span):
        at, mine = place(j)
        for t, (own, other) in enumerate(((own_normed, other_normed), (own_plain, other_plain))):
            for u in range(2):
                a = own[at, u * BLOCK : (u + 1) * BLOCK, :]
                b = other[at, u * BLOCK : (u + 1) * BLOCK, :]
                win[2 * t + u, j * BLOCK : (j + 1) * BLOCK, :] = jnp.where(mine, a, b)

    def clip_of(offset, shape, axis):
        token = lax.rem(first * BLOCK + offset + lax.broadcasted_iota(jnp.int32, shape, axis), total)
        clip = jnp.zeros(shape, jnp.int32)
        for end in ends:
            clip = clip + (token >= end).astype(jnp.int32)
        return clip, (clip == long_clip) == (core == 0)

    key_clip, key_valid = clip_of(0, (1, width), 1)
    key_clip = jnp.where(key_valid, key_clip, -1)
    keys = win[1]
    values = win[2]
    rows = 3 * BLOCK
    for ref in (own_av, other_av, own_qk, other_qk, own_inner, other_inner):
        ref[...] = jnp.zeros_like(ref)
    query_gain = jnp.zeros((1, HEAD_DIM), jnp.float32)

    def put(j, t, own, other, block_value, products=None):
        at, mine = place(j)
        if products is not None:
            row = jnp.sum(products.T, axis=0, keepdims=True)

        def store(out, inner):
            out[at, t * BLOCK : (t + 1) * BLOCK, :] = block_value
            if products is not None:
                inner[pl.ds(t * (blocks // 2) + at, 1), :] = row

        @pl.when(mine)
        def _():
            store(own, own_inner)

        @pl.when(jnp.logical_not(mine))
        def _():
            store(other, other_inner)

    nt = (((1,), (1,)), ((), ()))
    tn = (((0,), (0,)), ((), ()))
    for i in range(width // rows):
        query = win[0, i * rows : (i + 1) * rows, :]
        grad = win[3, i * rows : (i + 1) * rows, :]
        row_clip, row_valid = clip_of(i * rows, (rows, 1), 0)
        row_clip = jnp.where(row_valid, row_clip, -2)
        scores = lax.dot_general(query, keys, nt, preferred_element_type=jnp.float32)
        scores = jnp.where(row_clip == key_clip, scores * (scale * math.log2(math.e)), masked_score)
        row_max = jnp.max(scores, axis=1, keepdims=True)
        weights = jnp.exp2(scores - row_max)
        row_total = jnp.sum(weights, axis=1, keepdims=True)
        row_inv = jnp.where(row_valid, 1.0 / row_total, 0.0)
        low = weights.astype(jnp.bfloat16)
        attended = jnp.dot(low, values, preferred_element_type=jnp.float32) * row_inv
        grad_part = (grad.astype(jnp.float32) * row_inv).astype(jnp.bfloat16)
        dots = lax.dot_general(grad_part, values, nt, preferred_element_type=jnp.float32)
        delta = jnp.sum(weights * dots, axis=1, keepdims=True) * row_inv
        grad_scores = (weights * (dots - delta)).astype(jnp.bfloat16)
        query_norm_grad = jnp.dot(grad_scores, keys, preferred_element_type=jnp.float32) * scale
        value_part = lax.dot_general(low, grad_part, tn, preferred_element_type=jnp.float32)
        key_part = lax.dot_general(grad_scores, query, tn, preferred_element_type=jnp.float32)
        if i == 0:
            vacc[...] = value_part
            kacc[...] = key_part
        else:
            vacc[...] += value_part
            kacc[...] += key_part
        products = query_norm_grad * query.astype(jnp.float32)
        query_gain = query_gain + jnp.sum(products, axis=0, keepdims=True)
        attended = attended.astype(jnp.bfloat16)
        query_norm_grad = query_norm_grad.astype(jnp.bfloat16)
        for r in range(rows // BLOCK):
            part = slice(r * BLOCK, (r + 1) * BLOCK)
            put(i * (rows // BLOCK) + r, 0, own_qk, other_qk, query_norm_grad[part], products[part])
            put(i * (rows // BLOCK) + r, 0, own_av, other_av, attended[part])
    key_norm_grad = kacc[...] * scale
    products = key_norm_grad * keys.astype(jnp.float32)
    key_gain = jnp.sum(products, axis=0, keepdims=True)
    key_norm_grad = key_norm_grad.astype(jnp.bfloat16)
    value_grad = vacc[...].astype(jnp.bfloat16)
    for j in range(span):
        part = slice(j * BLOCK, (j + 1) * BLOCK)
        put(j, 1, own_qk, other_qk, key_norm_grad[part], products[part])
        put(j, 1, own_av, other_av, value_grad[part])

    zero = jnp.zeros((4, HEAD_DIM), jnp.float32)
    four = jnp.concatenate(halves(query_gain) + halves(key_gain), axis=0)
    here = jnp.concatenate([four, zero, zero, zero], axis=0).astype(jnp.bfloat16)
    there = jnp.concatenate([zero, four, zero, zero], axis=0).astype(jnp.bfloat16)
    for at in range(blocks // 2):
        own_av[at, 2 * BLOCK :, :] = here
        other_av[at, 2 * BLOCK :, :] = there


def halves(floats):
    high = floats.astype(jnp.bfloat16).astype(jnp.float32)
    return [high, floats - high]


def merge_kernel(own, other, inner, out):
    chips = own.shape[0]
    high, rest = halves(jnp.sum(inner[...], axis=0))
    pad = jnp.zeros((12, HEAD_DIM), jnp.float32)
    for at in range(chips):
        out[at, 0 : 2 * BLOCK, :] = own[at] + other[at]
        lines = [part[t * chips + at : t * chips + at + 1] for t in range(2) for part in (high, rest)]
        out[at, 2 * BLOCK :, :] = jnp.concatenate([*lines, pad], axis=0).astype(jnp.bfloat16)


def final_kernel(
    total_width, queries, keys, squares, query_gain, key_gain, av, qk, attended, query_grad, key_grad, value_grad
):
    heads = queries.shape[2] // HEAD_DIM
    invs = inverses(squares, total_width)
    lines = jnp.sum(qk[0:heads, 2 * BLOCK :, :].astype(jnp.float32), axis=0)
    for t, (ref, gain, grad) in enumerate(((queries, query_gain, query_grad), (keys, key_gain, key_grad))):
        inner = as_column(lines[2 * t : 2 * t + 1] + lines[2 * t + 1 : 2 * t + 2])
        factor = invs[t] * invs[t] * inner / total_width
        for h in range(heads):
            cols = slice(h * HEAD_DIM, (h + 1) * HEAD_DIM)
            norm_grad = qk[h, t * BLOCK : (t + 1) * BLOCK, :].astype(jnp.float32)
            grad[0, :, cols] = (
                invs[t] * gain[0:1, cols] * norm_grad - ref[0, :, cols].astype(jnp.float32) * factor
            ).astype(jnp.bfloat16)
    for h in range(heads):
        cols = slice(h * HEAD_DIM, (h + 1) * HEAD_DIM)
        attended[0, :, cols] = av[h, 0:BLOCK, :]
        value_grad[0, :, cols] = av[h, BLOCK : 2 * BLOCK, :]


def local(queries, keys, values, grad_out, lengths, query_gain, key_gain):
    rows, width = queries.shape[1:]
    total_width = width * lax.axis_size("section")
    seq = lax.axis_size("seq")
    chips = seq // 2
    same_core = [[2 * z + c for z in range(chips)] for c in range(2)]
    other_core = [(i, i ^ 1) for i in range(seq)]
    query_gain, key_gain = query_gain[None], key_gain[None]
    half_chunk = jax.ShapeDtypeStruct((chips, 2 * rows, HEAD_DIM), jnp.bfloat16)

    def to_heads(chunks):
        return lax.all_to_all(chunks, "seq", 0, 0, axis_index_groups=same_core, tiled=True)

    def swap(array):
        return lax.ppermute(array, "seq", other_core)

    plain = pl.pallas_call(
        pack_plain_kernel, out_shape=half_chunk, in_specs=[VMEM] * 2, out_specs=VMEM, name="pack_plain"
    )(values, grad_out)
    own_plain = to_heads(plain)
    other_plain = swap(own_plain)
    squares = pl.pallas_call(
        squares_kernel,
        out_shape=jax.ShapeDtypeStruct((8, rows), jnp.float32),
        in_specs=[VMEM] * 2,
        out_specs=VMEM,
        name="squares",
    )(queries, keys)
    squares = lax.all_gather(squares, "section")
    normed = pl.pallas_call(
        functools.partial(pack_normed_kernel, total_width),
        out_shape=half_chunk,
        in_specs=[VMEM] * 5,
        out_specs=VMEM,
        name="pack_normed",
    )(queries, keys, squares, query_gain, key_gain)
    own_normed = to_heads(normed)
    other_normed = swap(own_normed)

    window = (chips + 1) * BLOCK
    extra = 16
    long_chunk = jax.ShapeDtypeStruct((chips, 2 * rows + extra, HEAD_DIM), jnp.bfloat16)
    lines = jax.ShapeDtypeStruct((2 * chips, HEAD_DIM), jnp.float32)
    own_av, other_av, own_qk, other_qk, own_inner, other_inner = pl.pallas_call(
        functools.partial(attention_kernel, seq),
        out_shape=(long_chunk, long_chunk, half_chunk, half_chunk, lines, lines),
        in_specs=[SMEM] + [VMEM] * 4,
        out_specs=[VMEM] * 6,
        scratch_shapes=[
            pltpu.VMEM((4, window, HEAD_DIM), jnp.bfloat16),
            pltpu.VMEM((window, HEAD_DIM), jnp.float32),
            pltpu.VMEM((window, HEAD_DIM), jnp.float32),
        ],
        compiler_params=pltpu.CompilerParams(vmem_limit_bytes=48 * 2**20),
        cost_estimate=pl.CostEstimate(
            flops=12 * window * window * HEAD_DIM,
            transcendentals=window * window,
            bytes_accessed=16 * chips * rows * HEAD_DIM * 2,
        ),
        name="attention",
    )(lengths, own_normed, other_normed, own_plain, other_plain)

    av = own_av + swap(other_av)
    av, other_qk, own_inner, other_inner = lax.optimization_barrier((av, other_qk, own_inner, other_inner))
    av = to_heads(av)
    inner = lax.all_gather(own_inner + swap(other_inner), "section")
    qk = pl.pallas_call(
        merge_kernel, out_shape=long_chunk, in_specs=[VMEM] * 3, out_specs=VMEM, name="merge"
    )(own_qk, swap(other_qk), inner)
    qk = to_heads(qk)

    gains = av[: width // HEAD_DIM, 2 * rows : 2 * rows + 8].astype(jnp.float32)
    query_sum = (gains[:, 0] + gains[:, 1] + gains[:, 4] + gains[:, 5]).reshape(width)
    key_sum = (gains[:, 2] + gains[:, 3] + gains[:, 6] + gains[:, 7]).reshape(width)
    gains = lax.psum((query_sum / query_gain[0], key_sum / key_gain[0]), "dp")

    whole = jax.ShapeDtypeStruct((1, rows, width), jnp.bfloat16)
    grads = pl.pallas_call(
        functools.partial(final_kernel, total_width),
        out_shape=(whole, whole, whole, whole),
        in_specs=[VMEM] * 7,
        out_specs=[VMEM] * 4,
        name="final",
    )(queries, keys, squares, query_gain, key_gain, av, qk)
    return (*grads, *gains)


def solution(mesh):
    rows = P("dp", "seq", "section")
    features = P("section")
    return jax.shard_map(
        local,
        mesh=mesh,
        in_specs=(rows, rows, rows, rows, P("dp", None), features, features),
        out_specs=(rows, rows, rows, rows, features, features),
        check_vma=False,
    )
```

```python
import functools
import math

import jax
import jax.numpy as jnp
from jax import lax
from jax.experimental import pallas as pl
from jax.experimental.pallas import tpu as pltpu
from jax.sharding import PartitionSpec as P

HEAD_DIM = 128
BLOCK = 128
norm_eps = 1e-06
masked_score = -1e30

VMEM = pl.BlockSpec(memory_space=pltpu.VMEM)
SMEM = pl.BlockSpec(memory_space=pltpu.SMEM)


def as_row(column):
    return jnp.broadcast_to(column, (BLOCK, BLOCK)).T[0:1]


def as_column(row):
    return jnp.broadcast_to(row, (BLOCK, BLOCK)).T[:, 0:1]


def squares_kernel(queries, keys, out):
    out[...] = jnp.zeros_like(out)
    for t, ref in enumerate((queries, keys)):
        floats = ref[0].astype(jnp.float32)
        out[t : t + 1, :] = as_row(jnp.sum(floats * floats, axis=1, keepdims=True))


def inverses(squares, total_width):
    inverse = lax.rsqrt(squares[...] / total_width + norm_eps)
    return as_column(inverse[0:1]), as_column(inverse[1:2])


def pack_plain_kernel(first, second, out):
    heads = first.shape[2] // HEAD_DIM
    for h in range(heads):
        for t, ref in enumerate((first, second)):
            out[h, t * BLOCK : (t + 1) * BLOCK, :] = ref[0, :, h * HEAD_DIM : (h + 1) * HEAD_DIM]
    for h in range(heads, out.shape[0]):
        out[h] = jnp.zeros(out.shape[1:], out.dtype)


def pack_normed_kernel(total_width, queries, keys, squares, query_gain, key_gain, out):
    heads = queries.shape[2] // HEAD_DIM
    invs = inverses(squares, total_width)
    for t, (ref, gain) in enumerate(((queries, query_gain), (keys, key_gain))):
        for h in range(heads):
            cols = slice(h * HEAD_DIM, (h + 1) * HEAD_DIM)
            normed = ref[0, :, cols].astype(jnp.float32) * invs[t] * gain[0:1, cols]
            out[h, t * BLOCK : (t + 1) * BLOCK, :] = normed.astype(jnp.bfloat16)
    for h in range(heads, out.shape[0]):
        out[h] = jnp.zeros(out.shape[1:], out.dtype)


def attention_kernel(
    blocks,
    lengths,
    own_normed,
    other_normed,
    own_plain,
    other_plain,
    own_av,
    other_av,
    own_qk,
    other_qk,
    own_inner,
    other_inner,
    win,
    kacc,
    vacc,
):
    span = win.shape[1] // BLOCK
    width = span * BLOCK
    total = blocks * BLOCK
    scale = 1.0 / math.sqrt(HEAD_DIM)
    core = lax.rem(lax.axis_index("seq"), 2)
    ends = [lengths[0, 0]]
    long_clip = jnp.int32(0)
    begin = jnp.int32(0)
    for c in range(1, 4):
        is_long = lengths[0, c] == total // 2
        long_clip = jnp.where(is_long, c, long_clip)
        begin = jnp.where(is_long, ends[-1], begin)
        ends.append(ends[-1] + lengths[0, c])
    first = lax.rem(lax.div(begin, BLOCK) + core * (blocks // 2), blocks)

    def place(j):
        block = lax.rem(first + j, blocks)
        return lax.div(block, 2), lax.rem(block, 2) == core

    for j in range(span):
        at, mine = place(j)
        for t, (own, other) in enumerate(((own_normed, other_normed), (own_plain, other_plain))):
            for u in range(2):
                a = own[at, u * BLOCK : (u + 1) * BLOCK, :]
                b = other[at, u * BLOCK : (u + 1) * BLOCK, :]
                win[2 * t + u, j * BLOCK : (j + 1) * BLOCK, :] = jnp.where(mine, a, b)

    def clip_of(offset, shape, axis):
        token = lax.rem(first * BLOCK + offset + lax.broadcasted_iota(jnp.int32, shape, axis), total)
        clip = jnp.zeros(shape, jnp.int32)
        for end in ends:
            clip = clip + (token >= end).astype(jnp.int32)
        return clip, (clip == long_clip) == (core == 0)

    key_clip, key_valid = clip_of(0, (1, width), 1)
    key_clip = jnp.where(key_valid, key_clip, -1)
    keys = win[1]
    values = win[2]
    rows = 3 * BLOCK
    for ref in (own_av, other_av, own_qk, other_qk, own_inner, other_inner):
        ref[...] = jnp.zeros_like(ref)
    query_gain = jnp.zeros((1, HEAD_DIM), jnp.float32)

    def put(j, t, own, other, block_value, products=None):
        at, mine = place(j)
        if products is not None:
            row = jnp.sum(products.T, axis=0, keepdims=True)

        def store(out, inner):
            out[at, t * BLOCK : (t + 1) * BLOCK, :] = block_value
            if products is not None:
                inner[pl.ds(t * (blocks // 2) + at, 1), :] = row

        @pl.when(mine)
        def _():
            store(own, own_inner)

        @pl.when(jnp.logical_not(mine))
        def _():
            store(other, other_inner)

    nt = (((1,), (1,)), ((), ()))
    tn = (((0,), (0,)), ((), ()))
    for i in range(width // rows):
        query = win[0, i * rows : (i + 1) * rows, :]
        grad = win[3, i * rows : (i + 1) * rows, :]
        row_clip, row_valid = clip_of(i * rows, (rows, 1), 0)
        row_clip = jnp.where(row_valid, row_clip, -2)
        scores = lax.dot_general(query, keys, nt, preferred_element_type=jnp.float32)
        scores = jnp.where(row_clip == key_clip, scores * (scale * math.log2(math.e)), masked_score)
        row_max = jnp.max(scores, axis=1, keepdims=True)
        weights = jnp.exp2(scores - row_max)
        row_total = jnp.sum(weights, axis=1, keepdims=True)
        row_inv = jnp.where(row_valid, 1.0 / row_total, 0.0)
        low = weights.astype(jnp.bfloat16)
        attended = jnp.dot(low, values, preferred_element_type=jnp.float32) * row_inv
        grad_part = (grad.astype(jnp.float32) * row_inv).astype(jnp.bfloat16)
        dots = lax.dot_general(grad_part, values, nt, preferred_element_type=jnp.float32)
        delta = jnp.sum(weights * dots, axis=1, keepdims=True) * row_inv
        grad_scores = (weights * (dots - delta)).astype(jnp.bfloat16)
        query_norm_grad = jnp.dot(grad_scores, keys, preferred_element_type=jnp.float32) * scale
        value_part = lax.dot_general(low, grad_part, tn, preferred_element_type=jnp.float32)
        key_part = lax.dot_general(grad_scores, query, tn, preferred_element_type=jnp.float32)
        if i == 0:
            vacc[...] = value_part
            kacc[...] = key_part
        else:
            vacc[...] += value_part
            kacc[...] += key_part
        products = query_norm_grad * query.astype(jnp.float32)
        query_gain = query_gain + jnp.sum(products, axis=0, keepdims=True)
        attended = attended.astype(jnp.bfloat16)
        query_norm_grad = query_norm_grad.astype(jnp.bfloat16)
        for r in range(rows // BLOCK):
            part = slice(r * BLOCK, (r + 1) * BLOCK)
            put(i * (rows // BLOCK) + r, 0, own_qk, other_qk, query_norm_grad[part], products[part])
            put(i * (rows // BLOCK) + r, 0, own_av, other_av, attended[part])
    key_norm_grad = kacc[...] * scale
    products = key_norm_grad * keys.astype(jnp.float32)
    key_gain = jnp.sum(products, axis=0, keepdims=True)
    key_norm_grad = key_norm_grad.astype(jnp.bfloat16)
    value_grad = vacc[...].astype(jnp.bfloat16)
    for j in range(span):
        part = slice(j * BLOCK, (j + 1) * BLOCK)
        put(j, 1, own_qk, other_qk, key_norm_grad[part], products[part])
        put(j, 1, own_av, other_av, value_grad[part])

    zero = jnp.zeros((4, HEAD_DIM), jnp.float32)
    four = jnp.concatenate(halves(query_gain) + halves(key_gain), axis=0)
    here = jnp.concatenate([four, zero, zero, zero], axis=0).astype(jnp.bfloat16)
    there = jnp.concatenate([zero, four, zero, zero], axis=0).astype(jnp.bfloat16)
    for at in range(blocks // 2):
        own_av[at, 2 * BLOCK :, :] = here
        other_av[at, 2 * BLOCK :, :] = there


def halves(floats):
    high = floats.astype(jnp.bfloat16).astype(jnp.float32)
    return [high, floats - high]


def merge_kernel(own, other, inner, out):
    chips = own.shape[0]
    high, rest = halves(inner[...])
    pad = jnp.zeros((12, HEAD_DIM), jnp.float32)
    for at in range(chips):
        out[at, 0 : 2 * BLOCK, :] = own[at] + other[at]
        lines = [part[t * chips + at : t * chips + at + 1] for t in range(2) for part in (high, rest)]
        out[at, 2 * BLOCK :, :] = jnp.concatenate([*lines, pad], axis=0).astype(jnp.bfloat16)


def final_kernel(
    total_width, queries, keys, squares, query_gain, key_gain, av, qk, attended, query_grad, key_grad, value_grad
):
    heads = queries.shape[2] // HEAD_DIM
    invs = inverses(squares, total_width)
    lines = jnp.sum(qk[0:heads, 2 * BLOCK :, :].astype(jnp.float32), axis=0)
    for t, (ref, gain, grad) in enumerate(((queries, query_gain, query_grad), (keys, key_gain, key_grad))):
        inner = as_column(lines[2 * t : 2 * t + 1] + lines[2 * t + 1 : 2 * t + 2])
        factor = invs[t] * invs[t] * inner / total_width
        for h in range(heads):
            cols = slice(h * HEAD_DIM, (h + 1) * HEAD_DIM)
            norm_grad = qk[h, t * BLOCK : (t + 1) * BLOCK, :].astype(jnp.float32)
            grad[0, :, cols] = (
                invs[t] * gain[0:1, cols] * norm_grad - ref[0, :, cols].astype(jnp.float32) * factor
            ).astype(jnp.bfloat16)
    for h in range(heads):
        cols = slice(h * HEAD_DIM, (h + 1) * HEAD_DIM)
        attended[0, :, cols] = av[h, 0:BLOCK, :]
        value_grad[0, :, cols] = av[h, BLOCK : 2 * BLOCK, :]


def butterfly_sum(array, axis):
    step = 1
    size = lax.axis_size(axis)
    while step < size:
        array = array + lax.ppermute(array, axis, [(i, i ^ step) for i in range(size)])
        step *= 2
    return array


def local(queries, keys, values, grad_out, lengths, query_gain, key_gain):
    rows, width = queries.shape[1:]
    total_width = width * lax.axis_size("section")
    seq = lax.axis_size("seq")
    chips = seq // 2
    same_core = [[2 * z + c for z in range(chips)] for c in range(2)]
    other_core = [(i, i ^ 1) for i in range(seq)]
    query_gain, key_gain = query_gain[None], key_gain[None]
    half_chunk = jax.ShapeDtypeStruct((chips, 2 * rows, HEAD_DIM), jnp.bfloat16)

    def to_heads(chunks):
        return lax.all_to_all(chunks, "seq", 0, 0, axis_index_groups=same_core, tiled=True)

    def swap(array):
        return lax.ppermute(array, "seq", other_core)

    plain = pl.pallas_call(
        pack_plain_kernel, out_shape=half_chunk, in_specs=[VMEM] * 2, out_specs=VMEM, name="pack_plain"
    )(values, grad_out)
    own_plain = to_heads(plain)
    other_plain = swap(own_plain)
    squares = pl.pallas_call(
        squares_kernel,
        out_shape=jax.ShapeDtypeStruct((8, rows), jnp.float32),
        in_specs=[VMEM] * 2,
        out_specs=VMEM,
        name="squares",
    )(queries, keys)
    squares = butterfly_sum(squares, "section")
    normed = pl.pallas_call(
        functools.partial(pack_normed_kernel, total_width),
        out_shape=half_chunk,
        in_specs=[VMEM] * 5,
        out_specs=VMEM,
        name="pack_normed",
    )(queries, keys, squares, query_gain, key_gain)
    own_normed = to_heads(normed)
    other_normed = swap(own_normed)

    window = (chips + 1) * BLOCK
    extra = 16
    long_chunk = jax.ShapeDtypeStruct((chips, 2 * rows + extra, HEAD_DIM), jnp.bfloat16)
    lines = jax.ShapeDtypeStruct((2 * chips, HEAD_DIM), jnp.float32)
    own_av, other_av, own_qk, other_qk, own_inner, other_inner = pl.pallas_call(
        functools.partial(attention_kernel, seq),
        out_shape=(long_chunk, long_chunk, half_chunk, half_chunk, lines, lines),
        in_specs=[SMEM] + [VMEM] * 4,
        out_specs=[VMEM] * 6,
        scratch_shapes=[
            pltpu.VMEM((4, window, HEAD_DIM), jnp.bfloat16),
            pltpu.VMEM((window, HEAD_DIM), jnp.float32),
            pltpu.VMEM((window, HEAD_DIM), jnp.float32),
        ],
        compiler_params=pltpu.CompilerParams(vmem_limit_bytes=48 * 2**20),
        cost_estimate=pl.CostEstimate(
            flops=12 * window * window * HEAD_DIM,
            transcendentals=window * window,
            bytes_accessed=16 * chips * rows * HEAD_DIM * 2,
        ),
        name="attention",
    )(lengths, own_normed, other_normed, own_plain, other_plain)

    inner = own_inner + swap(other_inner)
    av = own_av + swap(other_av)
    av, other_qk, inner = lax.optimization_barrier((av, other_qk, inner))
    av = to_heads(av)
    inner = butterfly_sum(inner, "section")
    qk = pl.pallas_call(
        merge_kernel, out_shape=long_chunk, in_specs=[VMEM] * 3, out_specs=VMEM, name="merge"
    )(own_qk, swap(other_qk), inner)
    qk = to_heads(qk)

    gains = av[: width // HEAD_DIM, 2 * rows : 2 * rows + 8].astype(jnp.float32)
    query_sum = gains[:, 0] + gains[:, 1] + gains[:, 4] + gains[:, 5]
    key_sum = gains[:, 2] + gains[:, 3] + gains[:, 6] + gains[:, 7]
    gains = butterfly_sum(jnp.stack([query_sum, key_sum]), "dp").reshape(2, width)

    whole = jax.ShapeDtypeStruct((1, rows, width), jnp.bfloat16)
    grads = pl.pallas_call(
        functools.partial(final_kernel, total_width),
        out_shape=(whole, whole, whole, whole),
        in_specs=[VMEM] * 7,
        out_specs=[VMEM] * 4,
        name="final",
    )(queries, keys, squares, query_gain, key_gain, av, qk)
    return (*grads, gains[0] / query_gain[0], gains[1] / key_gain[0])


def solution(mesh):
    rows = P("dp", "seq", "section")
    features = P("section")
    return jax.shard_map(
        local,
        mesh=mesh,
        in_specs=(rows, rows, rows, rows, P("dp", None), features, features),
        out_specs=(rows, rows, rows, rows, features, features),
        check_vma=False,
    )
```

```python
import functools
import math

import jax
import jax.numpy as jnp
from jax import lax
from jax.experimental import pallas as pl
from jax.experimental.pallas import tpu as pltpu
from jax.sharding import PartitionSpec as P

HEAD_DIM = 128
BLOCK = 128
norm_eps = 1e-06
masked_score = -1e30

VMEM = pl.BlockSpec(memory_space=pltpu.VMEM)
SMEM = pl.BlockSpec(memory_space=pltpu.SMEM)


def as_row(column):
    return jnp.broadcast_to(column, (BLOCK, BLOCK)).T[0:1]


def as_column(row):
    return jnp.broadcast_to(row, (BLOCK, BLOCK)).T[:, 0:1]


def squares_kernel(queries, keys, out):
    out[...] = jnp.zeros_like(out)
    for t, ref in enumerate((queries, keys)):
        floats = ref[0].astype(jnp.float32)
        out[t : t + 1, :] = as_row(jnp.sum(floats * floats, axis=1, keepdims=True))


def inverses(squares, total_width):
    summed = jnp.sum(squares[...], axis=0)
    inverse = lax.rsqrt(summed / total_width + norm_eps)
    return as_column(inverse[0:1]), as_column(inverse[1:2])


def pack_kernel(*refs):
    *sources, out, sems = refs
    copies = []
    for t, ref in enumerate(sources):
        for h in range(ref.shape[2] // HEAD_DIM):
            copies.append(
                pltpu.make_async_copy(
                    ref.at[0, :, pl.ds(h * HEAD_DIM, HEAD_DIM)],
                    out.at[h, pl.ds(t * BLOCK, BLOCK), :],
                    sems.at[t, h],
                )
            )
    for copy in copies:
        copy.start()
    for copy in copies:
        copy.wait()


def attention_kernel(
    blocks,
    lengths,
    own,
    other,
    inverse,
    query_gain,
    key_gain,
    own_out,
    other_out,
    sums,
    win,
    kacc,
    vacc,
):
    span = win.shape[1] // BLOCK
    width = span * BLOCK
    total = blocks * BLOCK
    scale = 1.0 / math.sqrt(HEAD_DIM)
    core = lax.rem(lax.axis_index("seq"), 2)
    head = jnp.minimum(lax.div(lax.axis_index("seq"), 2), query_gain.shape[0] - 1)
    ends = [lengths[0, 0]]
    long_clip = jnp.int32(0)
    begin = jnp.int32(0)
    for c in range(1, 4):
        is_long = lengths[0, c] == total // 2
        long_clip = jnp.where(is_long, c, long_clip)
        begin = jnp.where(is_long, ends[-1], begin)
        ends.append(ends[-1] + lengths[0, c])
    first = lax.rem(lax.div(begin, BLOCK) + core * (blocks // 2), blocks)

    def place(j):
        block = lax.rem(first + j, blocks)
        return block, lax.div(block, 2), lax.rem(block, 2) == core

    gains = (query_gain[pl.ds(head, 1), :], key_gain[pl.ds(head, 1), :])
    for j in range(span):
        block, at, mine = place(j)
        for t in range(4):
            part = slice(t * BLOCK, (t + 1) * BLOCK)
            rows = jnp.where(mine, own[at, part, :], other[at, part, :])
            if t < 2:
                rows = rows.astype(jnp.float32) * as_column(inverse[block, t : t + 1, :]) * gains[t]
            win[t, j * BLOCK : (j + 1) * BLOCK, :] = rows.astype(jnp.bfloat16)

    def clip_of(offset, shape, axis):
        token = lax.rem(first * BLOCK + offset + lax.broadcasted_iota(jnp.int32, shape, axis), total)
        clip = jnp.zeros(shape, jnp.int32)
        for end in ends:
            clip = clip + (token >= end).astype(jnp.int32)
        return clip, (clip == long_clip) == (core == 0)

    key_clip, key_valid = clip_of(0, (1, width), 1)
    key_clip = jnp.where(key_valid, key_clip, -1)
    keys = win[1]
    values = win[2]
    rows = 3 * BLOCK
    for ref in (own_out, other_out, sums):
        ref[...] = jnp.zeros_like(ref)
    query_total = jnp.zeros((1, HEAD_DIM), jnp.float32)

    def put(j, t, block_value, products=None):
        block, at, mine = place(j)
        part = slice(t * BLOCK, (t + 1) * BLOCK)

        @pl.when(mine)
        def _():
            own_out[at, part, :] = block_value

        @pl.when(jnp.logical_not(mine))
        def _():
            other_out[at, part, :] = block_value

        if products is not None:
            sums[block, t : t + 1, :] = jnp.sum(products.T, axis=0, keepdims=True)

    nt = (((1,), (1,)), ((), ()))
    tn = (((0,), (0,)), ((), ()))
    for i in range(width // rows):
        query = win[0, i * rows : (i + 1) * rows, :]
        grad = win[3, i * rows : (i + 1) * rows, :]
        row_clip, row_valid = clip_of(i * rows, (rows, 1), 0)
        row_clip = jnp.where(row_valid, row_clip, -2)
        scores = lax.dot_general(query, keys, nt, preferred_element_type=jnp.float32)
        scores = jnp.where(row_clip == key_clip, scores * (scale * math.log2(math.e)), masked_score)
        row_max = jnp.max(scores, axis=1, keepdims=True)
        weights = jnp.exp2(scores - row_max)
        row_total = jnp.sum(weights, axis=1, keepdims=True)
        row_inv = jnp.where(row_valid, 1.0 / row_total, 0.0)
        low = weights.astype(jnp.bfloat16)
        attended = jnp.dot(low, values, preferred_element_type=jnp.float32) * row_inv
        grad_part = (grad.astype(jnp.float32) * row_inv).astype(jnp.bfloat16)
        dots = lax.dot_general(grad_part, values, nt, preferred_element_type=jnp.float32)
        delta = jnp.sum(weights * dots, axis=1, keepdims=True) * row_inv
        grad_scores = (weights * (dots - delta)).astype(jnp.bfloat16)
        query_norm_grad = jnp.dot(grad_scores, keys, preferred_element_type=jnp.float32) * scale
        value_part = lax.dot_general(low, grad_part, tn, preferred_element_type=jnp.float32)
        key_part = lax.dot_general(grad_scores, query, tn, preferred_element_type=jnp.float32)
        if i == 0:
            vacc[...] = value_part
            kacc[...] = key_part
        else:
            vacc[...] += value_part
            kacc[...] += key_part
        products = query_norm_grad * query.astype(jnp.float32)
        query_total = query_total + jnp.sum(products, axis=0, keepdims=True)
        attended = attended.astype(jnp.bfloat16)
        query_norm_grad = query_norm_grad.astype(jnp.bfloat16)
        for r in range(rows // BLOCK):
            part = slice(r * BLOCK, (r + 1) * BLOCK)
            put(i * (rows // BLOCK) + r, 0, query_norm_grad[part], products[part])
            put(i * (rows // BLOCK) + r, 2, attended[part])
    key_norm_grad = kacc[...] * scale
    products = key_norm_grad * keys.astype(jnp.float32)
    key_total = jnp.sum(products, axis=0, keepdims=True)
    key_norm_grad = key_norm_grad.astype(jnp.bfloat16)
    value_grad = vacc[...].astype(jnp.bfloat16)
    for j in range(span):
        part = slice(j * BLOCK, (j + 1) * BLOCK)
        put(j, 1, key_norm_grad[part], products[part])
        put(j, 3, value_grad[part])

    for block in range(blocks):
        sums[block, 2:3, :] = query_total
        sums[block, 3:4, :] = key_total


def final_kernel(
    total_width, queries, keys, squares, query_gain, key_gain, back, inner, attended, query_grad, key_grad, value_grad
):
    heads = queries.shape[2] // HEAD_DIM
    invs = inverses(squares, total_width)
    lines = jnp.sum(inner[...], axis=0)
    for t, (ref, gain, grad) in enumerate(((queries, query_gain, query_grad), (keys, key_gain, key_grad))):
        factor = invs[t] * invs[t] * as_column(lines[t : t + 1]) / total_width
        for h in range(heads):
            cols = slice(h * HEAD_DIM, (h + 1) * HEAD_DIM)
            norm_grad = back[h, t * BLOCK : (t + 1) * BLOCK, :].astype(jnp.float32)
            grad[0, :, cols] = (
                invs[t] * gain[h : h + 1, :] * norm_grad - ref[0, :, cols].astype(jnp.float32) * factor
            ).astype(jnp.bfloat16)
    for h in range(heads):
        cols = slice(h * HEAD_DIM, (h + 1) * HEAD_DIM)
        attended[0, :, cols] = back[h, 2 * BLOCK : 3 * BLOCK, :]
        value_grad[0, :, cols] = back[h, 3 * BLOCK : 4 * BLOCK, :]


def local(queries, keys, values, grad_out, lengths, query_gain, key_gain):
    rows, width = queries.shape[1:]
    heads = width // HEAD_DIM
    total_width = width * lax.axis_size("section")
    seq = lax.axis_size("seq")
    chips = seq // 2
    same_core = [[2 * z + c for z in range(chips)] for c in range(2)]
    other_core = [(i, i ^ 1) for i in range(seq)]
    query_gain, key_gain = query_gain.reshape(heads, HEAD_DIM), key_gain.reshape(heads, HEAD_DIM)
    chunk = jax.ShapeDtypeStruct((chips, 4 * rows, HEAD_DIM), jnp.bfloat16)
    hbm = pl.BlockSpec(memory_space=pl.ANY)

    def exchange(chunks):
        return lax.all_to_all(chunks, "seq", 0, 0, axis_index_groups=same_core, tiled=True)

    def swap(array):
        return lax.ppermute(array, "seq", other_core)

    packed = pl.pallas_call(
        pack_kernel,
        out_shape=chunk,
        in_specs=[hbm] * 4,
        out_specs=hbm,
        scratch_shapes=[pltpu.SemaphoreType.DMA((4, heads))],
        name="pack",
    )(queries, keys, values, grad_out)
    own = exchange(packed)
    squares = pl.pallas_call(
        squares_kernel,
        out_shape=jax.ShapeDtypeStruct((8, rows), jnp.float32),
        in_specs=[VMEM] * 2,
        out_specs=VMEM,
        name="squares",
    )(queries, keys)
    squares = lax.all_gather(squares, "section")
    inverse = lax.rsqrt(jnp.sum(squares, axis=0) / total_width + norm_eps)
    inverse = jnp.broadcast_to(inverse, (seq, 8, rows))
    own, inverse = lax.optimization_barrier((own, inverse))
    other = swap(own)
    inverse = lax.all_to_all(inverse, "seq", 0, 0, tiled=True)

    window = (chips + 1) * BLOCK
    own_out, other_out, sums = pl.pallas_call(
        functools.partial(attention_kernel, seq),
        out_shape=(chunk, chunk, jax.ShapeDtypeStruct((seq, 8, HEAD_DIM), jnp.float32)),
        in_specs=[SMEM] + [VMEM] * 5,
        out_specs=[VMEM] * 3,
        scratch_shapes=[
            pltpu.VMEM((4, window, HEAD_DIM), jnp.bfloat16),
            pltpu.VMEM((window, HEAD_DIM), jnp.float32),
            pltpu.VMEM((window, HEAD_DIM), jnp.float32),
        ],
        compiler_params=pltpu.CompilerParams(vmem_limit_bytes=48 * 2**20),
        cost_estimate=pl.CostEstimate(
            flops=12 * window * window * HEAD_DIM,
            transcendentals=window * window,
            bytes_accessed=16 * chips * rows * HEAD_DIM * 2,
        ),
        name="attention",
    )(lengths, own, other, inverse, query_gain, key_gain)

    other_out = swap(other_out)
    sums = lax.all_to_all(sums, "seq", 0, 0, tiled=True)
    sums, other_out = lax.optimization_barrier((sums, other_out))
    back = exchange(own_out + other_out)
    sums = jnp.sum(sums[: 2 * heads, 0:4].reshape(heads, 2, 4, HEAD_DIM), axis=1)
    inner = lax.all_gather(jnp.sum(sums[:, 0:2], axis=0), "section")
    gains = lax.psum((sums[:, 2] / query_gain, sums[:, 3] / key_gain), "dp")

    whole = jax.ShapeDtypeStruct((1, rows, width), jnp.bfloat16)
    grads = pl.pallas_call(
        functools.partial(final_kernel, total_width),
        out_shape=(whole, whole, whole, whole),
        in_specs=[VMEM] * 7,
        out_specs=[VMEM] * 4,
        name="final",
    )(queries, keys, squares, query_gain, key_gain, back, inner)
    return (*grads, gains[0].reshape(width), gains[1].reshape(width))


def solution(mesh):
    rows = P("dp", "seq", "section")
    features = P("section")
    return jax.shard_map(
        local,
        mesh=mesh,
        in_specs=(rows, rows, rows, rows, P("dp", None), features, features),
        out_specs=(rows, rows, rows, rows, features, features),
        check_vma=False,
    )
```

```python
import functools
import math

import jax
import jax.numpy as jnp
from jax import lax
from jax.experimental import pallas as pl
from jax.experimental.pallas import tpu as pltpu
from jax.sharding import PartitionSpec as P

HEAD_DIM = 128
BLOCK = 128
norm_eps = 1e-06
masked_score = -1e30

VMEM = pl.BlockSpec(memory_space=pltpu.VMEM)
SMEM = pl.BlockSpec(memory_space=pltpu.SMEM)


def as_row(column):
    return jnp.broadcast_to(column, (BLOCK, BLOCK)).T[0:1]


def as_column(row):
    return jnp.broadcast_to(row, (BLOCK, BLOCK)).T[:, 0:1]


def squares_kernel(queries, keys, out):
    out[...] = jnp.zeros_like(out)
    for t, ref in enumerate((queries, keys)):
        floats = ref[0].astype(jnp.float32)
        out[t : t + 1, :] = as_row(jnp.sum(floats * floats, axis=1, keepdims=True))


def inverses(squares, total_width):
    summed = jnp.sum(squares[...], axis=0)
    inverse = lax.rsqrt(summed / total_width + norm_eps)
    return as_column(inverse[0:1]), as_column(inverse[1:2])


def pack_kernel(*refs):
    *sources, out = refs
    for t, ref in enumerate(sources):
        out[0, t * BLOCK : (t + 1) * BLOCK, :] = ref[0]


def halves(floats):
    high = floats.astype(jnp.bfloat16).astype(jnp.float32)
    return [high, floats - high]


def attention_kernel(
    blocks,
    lengths,
    own,
    other,
    inverse,
    query_gain,
    key_gain,
    own_out,
    other_out,
    sums,
    win,
    kacc,
    vacc,
    res,
):
    span = win.shape[1] // BLOCK
    width = span * BLOCK
    total = blocks * BLOCK
    scale = 1.0 / math.sqrt(HEAD_DIM)
    core = lax.rem(lax.axis_index("seq"), 2)
    head = jnp.minimum(lax.div(lax.axis_index("seq"), 2), query_gain.shape[0] - 1)
    ends = [lengths[0, 0]]
    long_clip = jnp.int32(0)
    begin = jnp.int32(0)
    for c in range(1, 4):
        is_long = lengths[0, c] == total // 2
        long_clip = jnp.where(is_long, c, long_clip)
        begin = jnp.where(is_long, ends[-1], begin)
        ends.append(ends[-1] + lengths[0, c])
    first = lax.rem(lax.div(begin, BLOCK) + core * (blocks // 2), blocks)

    def place(j):
        block = lax.rem(first + j, blocks)
        return block, lax.div(block, 2), lax.rem(block, 2) == core

    fold = scale * math.log2(math.e)
    gains = (query_gain[pl.ds(head, 1), :] * fold, key_gain[pl.ds(head, 1), :])
    for j in range(span):
        block, at, mine = place(j)
        for t in range(4):
            part = slice(t * BLOCK, (t + 1) * BLOCK)
            rows = jnp.where(mine, own[at, part, :], other[at, part, :])
            if t < 2:
                rows = rows.astype(jnp.float32) * as_column(inverse[block, t : t + 1, :]) * gains[t]
            win[t, j * BLOCK : (j + 1) * BLOCK, :] = rows.astype(jnp.bfloat16)

    def clip_of(offset, shape, axis):
        token = lax.rem(first * BLOCK + offset + lax.broadcasted_iota(jnp.int32, shape, axis), total)
        clip = jnp.zeros(shape, jnp.int32)
        for end in ends:
            clip = clip + (token >= end).astype(jnp.int32)
        return clip, (clip == long_clip) == (core == 0)

    key_clip, key_valid = clip_of(0, (1, width), 1)
    key_clip = jnp.where(key_valid, key_clip, -1)
    keys = win[1]
    values = win[2]
    rows = 3 * BLOCK
    for ref in (own_out, other_out, sums):
        ref[...] = jnp.zeros_like(ref)
    query_total = jnp.zeros((1, HEAD_DIM), jnp.float32)

    nt = (((1,), (1,)), ((), ()))
    tn = (((0,), (0,)), ((), ()))
    ones = jnp.ones((8, HEAD_DIM), jnp.bfloat16)

    def row_sums(products):
        return sum(
            lax.dot_general(ones, part.astype(jnp.bfloat16), nt, preferred_element_type=jnp.float32)[0:1]
            for part in halves(products)
        )

    def put_sums(start, t, products):
        row = row_sums(products)
        for r in range(products.shape[0] // BLOCK):
            block = lax.rem(first + start // BLOCK + r, blocks)
            sums[block, t : t + 1, :] = row[:, r * BLOCK : (r + 1) * BLOCK]

    for i in range(width // rows):
        part = slice(i * rows, (i + 1) * rows)
        query = win[0, part, :]
        grad = win[3, part, :].astype(jnp.float32)
        row_clip, row_valid = clip_of(i * rows, (rows, 1), 0)
        row_clip = jnp.where(row_valid, row_clip, -2)
        scores = lax.dot_general(query, keys, nt, preferred_element_type=jnp.float32)
        scores = jnp.where(row_clip == key_clip, scores, masked_score)
        row_max = jnp.max(scores, axis=1, keepdims=True)
        weights = jnp.exp2(scores - row_max)
        row_total = jnp.sum(weights, axis=1, keepdims=True)
        row_inv = jnp.where(row_valid, 1.0 / row_total, 0.0)
        low = weights.astype(jnp.bfloat16)
        attended = (jnp.dot(low, values, preferred_element_type=jnp.float32) * row_inv).astype(jnp.bfloat16)
        grad = grad * row_inv
        delta = jnp.sum(grad * attended.astype(jnp.float32), axis=1, keepdims=True)
        grad = grad.astype(jnp.bfloat16)
        dots = lax.dot_general(grad, values, nt, preferred_element_type=jnp.float32)
        grad_scores = (weights * (dots - delta)).astype(jnp.bfloat16)
        query_norm_grad = jnp.dot(grad_scores, keys, preferred_element_type=jnp.float32) * scale
        value_part = lax.dot_general(low, grad, tn, preferred_element_type=jnp.float32)
        key_part = lax.dot_general(grad_scores, query, tn, preferred_element_type=jnp.float32)
        if i == 0:
            vacc[...] = value_part
            kacc[...] = key_part
        else:
            vacc[...] += value_part
            kacc[...] += key_part
        products = query_norm_grad * (query.astype(jnp.float32) * (1.0 / fold))
        query_total = query_total + jnp.sum(products, axis=0, keepdims=True)
        put_sums(i * rows, 0, products)
        res[0, part, :] = query_norm_grad.astype(jnp.bfloat16)
        res[2, part, :] = attended
    key_norm_grad = kacc[...] * (scale / fold)
    products = key_norm_grad * keys.astype(jnp.float32)
    key_total = jnp.sum(products, axis=0, keepdims=True)
    put_sums(0, 1, products)
    res[1] = key_norm_grad.astype(jnp.bfloat16)
    res[3] = vacc[...].astype(jnp.bfloat16)

    for j in range(span):
        _, at, mine = place(j)

        def store(out, at=at, j=j):
            for t in range(4):
                out[at, t * BLOCK : (t + 1) * BLOCK, :] = res[t, j * BLOCK : (j + 1) * BLOCK, :]

        pl.when(mine)(functools.partial(store, own_out))
        pl.when(jnp.logical_not(mine))(functools.partial(store, other_out))

    for block in range(blocks):
        sums[block, 2:3, :] = query_total
        sums[block, 3:4, :] = key_total


def final_kernel(
    total_width,
    queries,
    keys,
    squares,
    query_gain,
    key_gain,
    back,
    inner,
    attended,
    query_grad,
    key_grad,
    value_grad,
    invs,
    factors,
):
    head = pl.program_id(0)

    @pl.when(head == 0)
    def _():
        lines = jnp.sum(inner[...], axis=0)
        for t, inverse in enumerate(inverses(squares, total_width)):
            invs[t] = jnp.broadcast_to(inverse, (BLOCK, HEAD_DIM))
            factor = inverse * inverse * as_column(lines[t : t + 1]) / total_width
            factors[t] = jnp.broadcast_to(factor, (BLOCK, HEAD_DIM))

    for t, (ref, gain, grad) in enumerate(((queries, query_gain, query_grad), (keys, key_gain, key_grad))):
        norm_grad = back[0, t * BLOCK : (t + 1) * BLOCK, :].astype(jnp.float32)
        scaled = invs[t] * gain[pl.ds(head, 1), :] * norm_grad
        grad[0] = (scaled - ref[0].astype(jnp.float32) * factors[t]).astype(jnp.bfloat16)
    attended[0] = back[0, 2 * BLOCK : 3 * BLOCK, :]
    value_grad[0] = back[0, 3 * BLOCK : 4 * BLOCK, :]


def local(queries, keys, values, grad_out, lengths, query_gain, key_gain):
    rows, width = queries.shape[1:]
    heads = width // HEAD_DIM
    total_width = width * lax.axis_size("section")
    seq = lax.axis_size("seq")
    chips = seq // 2
    same_core = [[2 * z + c for z in range(chips)] for c in range(2)]
    other_core = [(i, i ^ 1) for i in range(seq)]
    query_gain, key_gain = query_gain.reshape(heads, HEAD_DIM), key_gain.reshape(heads, HEAD_DIM)
    chunk = jax.ShapeDtypeStruct((chips, 4 * rows, HEAD_DIM), jnp.bfloat16)

    def exchange(chunks):
        return lax.all_to_all(chunks, "seq", 0, 0, axis_index_groups=same_core, tiled=True)

    def swap(array):
        return lax.ppermute(array, "seq", other_core)

    columns = pl.BlockSpec((1, rows, HEAD_DIM), lambda h: (0, 0, h))
    head_chunk = pl.BlockSpec((1, 4 * rows, HEAD_DIM), lambda h: (h, 0, 0))
    packed = pl.pallas_call(
        pack_kernel,
        out_shape=chunk,
        grid=(heads,),
        in_specs=[columns] * 4,
        out_specs=head_chunk,
        name="pack",
    )(queries, keys, values, grad_out)
    own = exchange(packed)
    squares = pl.pallas_call(
        squares_kernel,
        out_shape=jax.ShapeDtypeStruct((8, rows), jnp.float32),
        in_specs=[VMEM] * 2,
        out_specs=VMEM,
        name="squares",
    )(queries, keys)
    squares = lax.all_gather(squares, "section")
    inverse = lax.rsqrt(jnp.sum(squares, axis=0) / total_width + norm_eps)
    inverse = jnp.broadcast_to(inverse, (seq, 8, rows))
    own, inverse = lax.optimization_barrier((own, inverse))
    other = swap(own)
    inverse = lax.all_to_all(inverse, "seq", 0, 0, tiled=True)

    window = (chips + 1) * BLOCK
    own_out, other_out, sums = pl.pallas_call(
        functools.partial(attention_kernel, seq),
        out_shape=(chunk, chunk, jax.ShapeDtypeStruct((seq, 8, HEAD_DIM), jnp.float32)),
        in_specs=[SMEM] + [VMEM] * 5,
        out_specs=[VMEM] * 3,
        scratch_shapes=[
            pltpu.VMEM((4, window, HEAD_DIM), jnp.bfloat16),
            pltpu.VMEM((window, HEAD_DIM), jnp.float32),
            pltpu.VMEM((window, HEAD_DIM), jnp.float32),
            pltpu.VMEM((4, window, HEAD_DIM), jnp.bfloat16),
        ],
        compiler_params=pltpu.CompilerParams(vmem_limit_bytes=48 * 2**20),
        cost_estimate=pl.CostEstimate(
            flops=12 * window * window * HEAD_DIM,
            transcendentals=window * window,
            bytes_accessed=16 * chips * rows * HEAD_DIM * 2,
        ),
        name="attention",
    )(lengths, own, other, inverse, query_gain, key_gain)

    other_out = swap(other_out)
    sums = lax.all_to_all(sums, "seq", 0, 0, tiled=True)
    sums, other_out = lax.optimization_barrier((sums, other_out))
    back = exchange(own_out + other_out)
    sums = jnp.sum(sums[: 2 * heads, 0:4].reshape(heads, 2, 4, HEAD_DIM), axis=1)
    inner = lax.all_gather(jnp.sum(sums[:, 0:2], axis=0), "section")
    gains = lax.psum((sums[:, 2] / query_gain, sums[:, 3] / key_gain), "dp")

    whole = jax.ShapeDtypeStruct((1, rows, width), jnp.bfloat16)
    grads = pl.pallas_call(
        functools.partial(final_kernel, total_width),
        out_shape=(whole, whole, whole, whole),
        grid=(heads,),
        in_specs=[columns, columns, VMEM, VMEM, VMEM, head_chunk, VMEM],
        out_specs=[columns] * 4,
        scratch_shapes=[pltpu.VMEM((2, rows, HEAD_DIM), jnp.float32)] * 2,
        name="final",
    )(queries, keys, squares, query_gain, key_gain, back, inner)
    return (*grads, gains[0].reshape(width), gains[1].reshape(width))


def solution(mesh):
    rows = P("dp", "seq", "section")
    features = P("section")
    return jax.shard_map(
        local,
        mesh=mesh,
        in_specs=(rows, rows, rows, rows, P("dp", None), features, features),
        out_specs=(rows, rows, rows, rows, features, features),
        check_vma=False,
    )
```

```python
import functools
import math

import jax
import jax.numpy as jnp
from jax import lax
from jax.experimental import pallas as pl
from jax.experimental.pallas import tpu as pltpu
from jax.sharding import PartitionSpec as P

HEAD_DIM = 128
BLOCK = 128
norm_eps = 1e-06
masked_score = -1e30

VMEM = pl.BlockSpec(memory_space=pltpu.VMEM)
SMEM = pl.BlockSpec(memory_space=pltpu.SMEM)


def as_row(column):
    return jnp.broadcast_to(column, (BLOCK, BLOCK)).T[0:1]


def as_column(row):
    return jnp.broadcast_to(row, (BLOCK, BLOCK)).T[:, 0:1]


def squares_kernel(queries, keys, out):
    out[...] = jnp.zeros_like(out)
    for t, ref in enumerate((queries, keys)):
        floats = ref[0].astype(jnp.float32)
        out[t : t + 1, :] = as_row(jnp.sum(floats * floats, axis=1, keepdims=True))


def inverses(squares, total_width):
    summed = jnp.sum(squares[...], axis=0)
    inverse = lax.rsqrt(summed / total_width + norm_eps)
    return as_column(inverse[0:1]), as_column(inverse[1:2])


def pack_kernel(total_width, queries, keys, squares, query_gain, key_gain, values, grad_out, out, buffer, sems):
    copies = []
    invs = [jnp.broadcast_to(inverse, (BLOCK, HEAD_DIM)) for inverse in inverses(squares, total_width)]
    for h in range(query_gain.shape[0]):
        cols = slice(h * HEAD_DIM, (h + 1) * HEAD_DIM)
        for t, (ref, gain) in enumerate(((queries, query_gain), (keys, key_gain))):
            normed = ref[0, :, cols].astype(jnp.float32) * invs[t] * gain[h : h + 1, :]
            buffer[h, t * BLOCK : (t + 1) * BLOCK, :] = normed.astype(jnp.bfloat16)
        for t, ref in enumerate((values, grad_out)):
            buffer[h, (2 + t) * BLOCK : (3 + t) * BLOCK, :] = ref[0, :, cols]
        copies.append(pltpu.make_async_copy(buffer.at[h], out.at[h], sems.at[h]))
        copies[-1].start()
    for copy in copies:
        copy.wait()


def halves(floats):
    high = floats.astype(jnp.bfloat16).astype(jnp.float32)
    return [high, floats - high]


def attention_kernel(
    blocks,
    lengths,
    own,
    other,
    own_out,
    other_out,
    sums,
    win,
    kacc,
    vacc,
    res,
):
    span = win.shape[1] // BLOCK
    width = span * BLOCK
    total = blocks * BLOCK
    scale = 1.0 / math.sqrt(HEAD_DIM)
    core = lax.rem(lax.axis_index("seq"), 2)
    ends = [lengths[0, 0]]
    long_clip = jnp.int32(0)
    begin = jnp.int32(0)
    for c in range(1, 4):
        is_long = lengths[0, c] == total // 2
        long_clip = jnp.where(is_long, c, long_clip)
        begin = jnp.where(is_long, ends[-1], begin)
        ends.append(ends[-1] + lengths[0, c])
    first = lax.rem(lax.div(begin, BLOCK) + core * (blocks // 2), blocks)

    def place(j):
        block = lax.rem(first + j, blocks)
        return block, lax.div(block, 2), lax.rem(block, 2) == core

    for j in range(span):
        _, at, mine = place(j)
        for t in range(4):
            part = slice(t * BLOCK, (t + 1) * BLOCK)
            win[t, j * BLOCK : (j + 1) * BLOCK, :] = jnp.where(mine, own[at, part, :], other[at, part, :])

    def clip_of(offset, shape, axis):
        token = lax.rem(first * BLOCK + offset + lax.broadcasted_iota(jnp.int32, shape, axis), total)
        clip = jnp.zeros(shape, jnp.int32)
        for end in ends:
            clip = clip + (token >= end).astype(jnp.int32)
        return clip, (clip == long_clip) == (core == 0)

    key_clip, key_valid = clip_of(0, (1, width), 1)
    key_clip = jnp.where(key_valid, key_clip, -1)
    keys = win[1]
    values = win[2]
    rows = 3 * BLOCK
    for ref in (own_out, other_out, sums):
        ref[...] = jnp.zeros_like(ref)
    query_total = jnp.zeros((1, HEAD_DIM), jnp.float32)

    nt = (((1,), (1,)), ((), ()))
    tn = (((0,), (0,)), ((), ()))
    ones = jnp.ones((8, HEAD_DIM), jnp.bfloat16)

    def row_sums(products):
        return sum(
            lax.dot_general(ones, part.astype(jnp.bfloat16), nt, preferred_element_type=jnp.float32)[0:1]
            for part in halves(products)
        )

    def put_sums(start, t, products):
        row = row_sums(products)
        for r in range(products.shape[0] // BLOCK):
            block = lax.rem(first + start // BLOCK + r, blocks)
            sums[block, t : t + 1, :] = row[:, r * BLOCK : (r + 1) * BLOCK]

    for i in range(width // rows):
        part = slice(i * rows, (i + 1) * rows)
        query = win[0, part, :]
        grad = win[3, part, :].astype(jnp.float32)
        row_clip, row_valid = clip_of(i * rows, (rows, 1), 0)
        row_clip = jnp.where(row_valid, row_clip, -2)
        scores = lax.dot_general(query, keys, nt, preferred_element_type=jnp.float32)
        scores = jnp.where(row_clip == key_clip, scores * (scale * math.log2(math.e)), masked_score)
        row_max = jnp.max(scores, axis=1, keepdims=True)
        weights = jnp.exp2(scores - row_max)
        row_total = jnp.sum(weights, axis=1, keepdims=True)
        row_inv = jnp.where(row_valid, 1.0 / row_total, 0.0)
        low = weights.astype(jnp.bfloat16)
        attended = (jnp.dot(low, values, preferred_element_type=jnp.float32) * row_inv).astype(jnp.bfloat16)
        grad = grad * row_inv
        delta = jnp.sum(grad * attended.astype(jnp.float32), axis=1, keepdims=True)
        grad = grad.astype(jnp.bfloat16)
        dots = lax.dot_general(grad, values, nt, preferred_element_type=jnp.float32)
        grad_scores = (weights * (dots - delta)).astype(jnp.bfloat16)
        query_norm_grad = jnp.dot(grad_scores, keys, preferred_element_type=jnp.float32) * scale
        value_part = lax.dot_general(low, grad, tn, preferred_element_type=jnp.float32)
        key_part = lax.dot_general(grad_scores, query, tn, preferred_element_type=jnp.float32)
        if i == 0:
            vacc[...] = value_part
            kacc[...] = key_part
        else:
            vacc[...] += value_part
            kacc[...] += key_part
        products = query_norm_grad * query.astype(jnp.float32)
        query_total = query_total + jnp.sum(products, axis=0, keepdims=True)
        put_sums(i * rows, 0, products)
        res[0, part, :] = query_norm_grad.astype(jnp.bfloat16)
        res[2, part, :] = attended
    key_norm_grad = kacc[...] * scale
    products = key_norm_grad * keys.astype(jnp.float32)
    key_total = jnp.sum(products, axis=0, keepdims=True)
    put_sums(0, 1, products)
    res[1] = key_norm_grad.astype(jnp.bfloat16)
    res[3] = vacc[...].astype(jnp.bfloat16)

    for j in range(span):
        _, at, mine = place(j)

        def store(out, at=at, j=j):
            for t in range(4):
                out[at, t * BLOCK : (t + 1) * BLOCK, :] = res[t, j * BLOCK : (j + 1) * BLOCK, :]

        pl.when(mine)(functools.partial(store, own_out))
        pl.when(jnp.logical_not(mine))(functools.partial(store, other_out))

    for block in range(blocks):
        sums[block, 2:3, :] = query_total
        sums[block, 3:4, :] = key_total


def final_kernel(
    total_width,
    queries,
    keys,
    squares,
    query_gain,
    key_gain,
    inner,
    back,
    attended,
    query_grad,
    key_grad,
    value_grad,
):
    heads = query_gain.shape[0]
    invs, factors = [], []
    lines = jnp.sum(inner[...], axis=0)
    for t, inverse in enumerate(inverses(squares, total_width)):
        invs.append(jnp.broadcast_to(inverse, (BLOCK, HEAD_DIM)))
        factor = inverse * inverse * as_column(lines[t : t + 1]) / total_width
        factors.append(jnp.broadcast_to(factor, (BLOCK, HEAD_DIM)))
    for h in range(heads):
        cols = slice(h * HEAD_DIM, (h + 1) * HEAD_DIM)
        for t, (ref, gain, grad) in enumerate(((queries, query_gain, query_grad), (keys, key_gain, key_grad))):
            norm_grad = back[h, t * BLOCK : (t + 1) * BLOCK, :].astype(jnp.float32)
            scaled = invs[t] * gain[h : h + 1, :] * norm_grad
            grad[0, :, cols] = (scaled - ref[0, :, cols].astype(jnp.float32) * factors[t]).astype(jnp.bfloat16)
        attended[0, :, cols] = back[h, 2 * BLOCK : 3 * BLOCK, :]
        value_grad[0, :, cols] = back[h, 3 * BLOCK : 4 * BLOCK, :]


def local(queries, keys, values, grad_out, lengths, query_gain, key_gain):
    rows, width = queries.shape[1:]
    heads = width // HEAD_DIM
    total_width = width * lax.axis_size("section")
    seq = lax.axis_size("seq")
    chips = seq // 2
    same_core = [[2 * z + c for z in range(chips)] for c in range(2)]
    other_core = [(i, i ^ 1) for i in range(seq)]
    query_gain, key_gain = query_gain.reshape(heads, HEAD_DIM), key_gain.reshape(heads, HEAD_DIM)
    chunk = jax.ShapeDtypeStruct((chips, 4 * rows, HEAD_DIM), jnp.bfloat16)

    def exchange(chunks):
        return lax.all_to_all(chunks, "seq", 0, 0, axis_index_groups=same_core, tiled=True)

    def swap(array):
        return lax.ppermute(array, "seq", other_core)

    small = pltpu.CompilerParams(vmem_limit_bytes=12 * 2**20)
    squares = pl.pallas_call(
        squares_kernel,
        out_shape=jax.ShapeDtypeStruct((8, rows), jnp.float32),
        in_specs=[VMEM] * 2,
        out_specs=VMEM,
        compiler_params=small,
        name="squares",
    )(queries, keys)
    squares = lax.all_gather(squares, "section")
    packed = pl.pallas_call(
        functools.partial(pack_kernel, total_width),
        out_shape=chunk,
        in_specs=[VMEM] * 7,
        out_specs=pl.BlockSpec(memory_space=pl.ANY),
        scratch_shapes=[
            pltpu.VMEM((heads, 4 * rows, HEAD_DIM), jnp.bfloat16),
            pltpu.SemaphoreType.DMA((heads,)),
        ],
        compiler_params=small,
        name="pack",
    )(queries, keys, squares, query_gain, key_gain, values, grad_out)
    own = exchange(packed)
    other = swap(own)

    window = (chips + 1) * BLOCK
    own_out, other_out, sums = pl.pallas_call(
        functools.partial(attention_kernel, seq),
        out_shape=(chunk, chunk, jax.ShapeDtypeStruct((seq, 8, HEAD_DIM), jnp.float32)),
        in_specs=[SMEM] + [VMEM] * 2,
        out_specs=[VMEM] * 3,
        scratch_shapes=[
            pltpu.VMEM((4, window, HEAD_DIM), jnp.bfloat16),
            pltpu.VMEM((window, HEAD_DIM), jnp.float32),
            pltpu.VMEM((window, HEAD_DIM), jnp.float32),
            pltpu.VMEM((4, window, HEAD_DIM), jnp.bfloat16),
        ],
        compiler_params=pltpu.CompilerParams(vmem_limit_bytes=40 * 2**20),
        cost_estimate=pl.CostEstimate(
            flops=12 * window * window * HEAD_DIM,
            transcendentals=window * window,
            bytes_accessed=16 * chips * rows * HEAD_DIM * 2,
        ),
        name="attention",
    )(lengths, own, other)

    other_out = swap(other_out)
    sums = lax.all_to_all(sums, "seq", 0, 0, tiled=True)
    sums, other_out = lax.optimization_barrier((sums, other_out))
    back = exchange(own_out + other_out)
    sums = jnp.sum(sums[: 2 * heads, 0:4].reshape(heads, 2, 4, HEAD_DIM), axis=1)
    inner = lax.all_gather(jnp.sum(sums[:, 0:2], axis=0), "section")
    gains = lax.psum((sums[:, 2] / query_gain, sums[:, 3] / key_gain), "dp")

    whole = jax.ShapeDtypeStruct((1, rows, width), jnp.bfloat16)
    grads = pl.pallas_call(
        functools.partial(final_kernel, total_width),
        out_shape=(whole, whole, whole, whole),
        in_specs=[VMEM] * 7,
        out_specs=[VMEM] * 4,
        compiler_params=small,
        name="final",
    )(queries, keys, squares, query_gain, key_gain, inner, back)
    return (*grads, gains[0].reshape(width), gains[1].reshape(width))


def solution(mesh):
    rows = P("dp", "seq", "section")
    features = P("section")
    return jax.shard_map(
        local,
        mesh=mesh,
        in_specs=(rows, rows, rows, rows, P("dp", None), features, features),
        out_specs=(rows, rows, rows, rows, features, features),
        check_vma=False,
    )
```

```python
import functools
import math

import jax
import jax.numpy as jnp
from jax import lax
from jax.experimental import pallas as pl
from jax.experimental.pallas import tpu as pltpu
from jax.sharding import PartitionSpec as P

HEAD_DIM = 128
BLOCK = 128
norm_eps = 1e-06
masked_score = -1e30

VMEM = pl.BlockSpec(memory_space=pltpu.VMEM)
SMEM = pl.BlockSpec(memory_space=pltpu.SMEM)


def as_row(column):
    return jnp.broadcast_to(column, (BLOCK, BLOCK)).T[0:1]


def as_column(row):
    return jnp.broadcast_to(row, (BLOCK, BLOCK)).T[:, 0:1]


def inverses(squares, total_width):
    summed = jnp.sum(squares[...], axis=0)
    inverse = lax.rsqrt(summed / total_width + norm_eps)
    return as_column(inverse[0:1]), as_column(inverse[1:2])


def pack_kernel(queries, keys, values, grad_out, out, squares, held, buffer, in_sems, out_sems):
    heads = buffer.shape[0]
    refs = (queries, keys, values, grad_out)
    arrive = [pltpu.make_async_copy(ref, held.at[t], in_sems.at[t]) for t, ref in enumerate(refs)]
    for copy in arrive:
        copy.start()
    leave = []
    for t in range(4):
        arrive[t].wait()
        lines = pl.ds(t * BLOCK, BLOCK)
        for h in range(heads):
            buffer[h, lines, :] = held[t, 0, :, h * HEAD_DIM : (h + 1) * HEAD_DIM]
        place = out.at[pl.ds(0, heads), lines, :]
        leave.append(pltpu.make_async_copy(buffer.at[:, lines, :], place, out_sems.at[t]))
        leave[t].start()
    squares[...] = jnp.zeros_like(squares)
    for t in range(2):
        floats = held[t, 0].astype(jnp.float32)
        squares[t : t + 1, :] = as_row(jnp.sum(floats * floats, axis=1, keepdims=True))
    for copy in leave:
        copy.wait()


def halves(floats):
    high = floats.astype(jnp.bfloat16).astype(jnp.float32)
    return [high, floats - high]


def attention_kernel(
    blocks,
    lengths,
    own,
    other,
    inverse,
    query_gain,
    key_gain,
    own_out,
    other_out,
    sums,
    win,
    kacc,
    vacc,
    res,
):
    span = win.shape[1] // BLOCK
    width = span * BLOCK
    total = blocks * BLOCK
    scale = 1.0 / math.sqrt(HEAD_DIM)
    core = lax.rem(lax.axis_index("seq"), 2)
    head = jnp.minimum(lax.div(lax.axis_index("seq"), 2), query_gain.shape[0] - 1)
    ends = [lengths[0, 0]]
    long_clip = jnp.int32(0)
    begin = jnp.int32(0)
    for c in range(1, 4):
        is_long = lengths[0, c] == total // 2
        long_clip = jnp.where(is_long, c, long_clip)
        begin = jnp.where(is_long, ends[-1], begin)
        ends.append(ends[-1] + lengths[0, c])
    first = lax.rem(lax.div(begin, BLOCK) + core * (blocks // 2), blocks)

    def place(j):
        block = lax.rem(first + j, blocks)
        return block, lax.div(block, 2), lax.rem(block, 2) == core

    fold = scale * math.log2(math.e)
    gains = (query_gain[pl.ds(head, 1), :] * fold, key_gain[pl.ds(head, 1), :])
    for j in range(span):
        block, at, mine = place(j)
        for t in range(4):
            part = slice(t * BLOCK, (t + 1) * BLOCK)
            rows = jnp.where(mine, own[at, part, :], other[at, part, :])
            if t < 2:
                rows = rows.astype(jnp.float32) * as_column(inverse[block, t : t + 1, :]) * gains[t]
            win[t, j * BLOCK : (j + 1) * BLOCK, :] = rows.astype(jnp.bfloat16)

    def clip_of(offset, shape, axis):
        token = lax.rem(first * BLOCK + offset + lax.broadcasted_iota(jnp.int32, shape, axis), total)
        clip = jnp.zeros(shape, jnp.int32)
        for end in ends:
            clip = clip + (token >= end).astype(jnp.int32)
        return clip, (clip == long_clip) == (core == 0)

    key_clip, key_valid = clip_of(0, (1, width), 1)
    key_clip = jnp.where(key_valid, key_clip, -1)
    keys = win[1]
    values = win[2]
    rows = 3 * BLOCK
    for ref in (own_out, other_out, sums):
        ref[...] = jnp.zeros_like(ref)
    query_total = jnp.zeros((1, HEAD_DIM), jnp.float32)

    nt = (((1,), (1,)), ((), ()))
    tn = (((0,), (0,)), ((), ()))
    ones = jnp.ones((8, HEAD_DIM), jnp.bfloat16)

    def row_sums(products):
        return sum(
            lax.dot_general(ones, part.astype(jnp.bfloat16), nt, preferred_element_type=jnp.float32)[0:1]
            for part in halves(products)
        )

    def put_sums(start, t, products):
        row = row_sums(products)
        for r in range(products.shape[0] // BLOCK):
            block = lax.rem(first + start // BLOCK + r, blocks)
            sums[block, t : t + 1, :] = row[:, r * BLOCK : (r + 1) * BLOCK]

    for i in range(width // rows):
        part = slice(i * rows, (i + 1) * rows)
        query = win[0, part, :]
        grad = win[3, part, :].astype(jnp.float32)
        row_clip, row_valid = clip_of(i * rows, (rows, 1), 0)
        row_clip = jnp.where(row_valid, row_clip, -2)
        scores = lax.dot_general(query, keys, nt, preferred_element_type=jnp.float32)
        scores = jnp.where(row_clip == key_clip, scores, masked_score)
        row_max = jnp.max(scores, axis=1, keepdims=True)
        weights = jnp.exp2(scores - row_max)
        row_total = jnp.sum(weights, axis=1, keepdims=True)
        row_inv = jnp.where(row_valid, 1.0 / row_total, 0.0)
        low = weights.astype(jnp.bfloat16)
        attended = (jnp.dot(low, values, preferred_element_type=jnp.float32) * row_inv).astype(jnp.bfloat16)
        grad = grad * row_inv
        delta = jnp.sum(grad * attended.astype(jnp.float32), axis=1, keepdims=True)
        grad = grad.astype(jnp.bfloat16)
        dots = lax.dot_general(grad, values, nt, preferred_element_type=jnp.float32)
        grad_scores = (weights * (dots - delta)).astype(jnp.bfloat16)
        query_norm_grad = jnp.dot(grad_scores, keys, preferred_element_type=jnp.float32) * scale
        value_part = lax.dot_general(low, grad, tn, preferred_element_type=jnp.float32)
        key_part = lax.dot_general(grad_scores, query, tn, preferred_element_type=jnp.float32)
        if i == 0:
            vacc[...] = value_part
            kacc[...] = key_part
        else:
            vacc[...] += value_part
            kacc[...] += key_part
        products = query_norm_grad * (query.astype(jnp.float32) * (1.0 / fold))
        query_total = query_total + jnp.sum(products, axis=0, keepdims=True)
        put_sums(i * rows, 0, products)
        res[0, part, :] = query_norm_grad.astype(jnp.bfloat16)
        res[2, part, :] = attended
    key_norm_grad = kacc[...] * (scale / fold)
    products = key_norm_grad * keys.astype(jnp.float32)
    key_total = jnp.sum(products, axis=0, keepdims=True)
    put_sums(0, 1, products)
    res[1] = key_norm_grad.astype(jnp.bfloat16)
    res[3] = vacc[...].astype(jnp.bfloat16)

    for j in range(span):
        _, at, mine = place(j)

        def store(out, at=at, j=j):
            for t in range(4):
                out[at, t * BLOCK : (t + 1) * BLOCK, :] = res[t, j * BLOCK : (j + 1) * BLOCK, :]

        pl.when(mine)(functools.partial(store, own_out))
        pl.when(jnp.logical_not(mine))(functools.partial(store, other_out))

    for block in range(blocks):
        sums[block, 2:3, :] = query_total
        sums[block, 3:4, :] = key_total


def final_kernel(
    total_width,
    queries,
    keys,
    squares,
    query_gain,
    key_gain,
    inner,
    back,
    attended,
    query_grad,
    key_grad,
    value_grad,
):
    heads = query_gain.shape[0]
    invs, factors = [], []
    lines = jnp.sum(inner[...], axis=0)
    for t, inverse in enumerate(inverses(squares, total_width)):
        invs.append(jnp.broadcast_to(inverse, (BLOCK, HEAD_DIM)))
        factor = inverse * inverse * as_column(lines[t : t + 1]) / total_width
        factors.append(jnp.broadcast_to(factor, (BLOCK, HEAD_DIM)))
    for h in range(heads):
        cols = slice(h * HEAD_DIM, (h + 1) * HEAD_DIM)
        for t, (ref, gain, grad) in enumerate(((queries, query_gain, query_grad), (keys, key_gain, key_grad))):
            norm_grad = back[h, t * BLOCK : (t + 1) * BLOCK, :].astype(jnp.float32)
            scaled = invs[t] * gain[h : h + 1, :] * norm_grad
            grad[0, :, cols] = (scaled - ref[0, :, cols].astype(jnp.float32) * factors[t]).astype(jnp.bfloat16)
        attended[0, :, cols] = back[h, 2 * BLOCK : 3 * BLOCK, :]
        value_grad[0, :, cols] = back[h, 3 * BLOCK : 4 * BLOCK, :]


def local(queries, keys, values, grad_out, lengths, query_gain, key_gain):
    rows, width = queries.shape[1:]
    heads = width // HEAD_DIM
    total_width = width * lax.axis_size("section")
    seq = lax.axis_size("seq")
    chips = seq // 2
    same_core = [[2 * z + c for z in range(chips)] for c in range(2)]
    other_core = [(i, i ^ 1) for i in range(seq)]
    query_gain, key_gain = query_gain.reshape(heads, HEAD_DIM), key_gain.reshape(heads, HEAD_DIM)
    chunk = jax.ShapeDtypeStruct((chips, 4 * rows, HEAD_DIM), jnp.bfloat16)

    def exchange(chunks):
        return lax.all_to_all(chunks, "seq", 0, 0, axis_index_groups=same_core, tiled=True)

    def swap(array):
        return lax.ppermute(array, "seq", other_core)

    hbm = pl.BlockSpec(memory_space=pl.ANY)
    packed, squares = pl.pallas_call(
        pack_kernel,
        out_shape=(chunk, jax.ShapeDtypeStruct((8, rows), jnp.float32)),
        in_specs=[hbm] * 4,
        out_specs=(hbm, VMEM),
        scratch_shapes=[
            pltpu.VMEM((4, 1, rows, width), jnp.bfloat16),
            pltpu.VMEM((heads, 4 * rows, HEAD_DIM), jnp.bfloat16),
            pltpu.SemaphoreType.DMA((4,)),
            pltpu.SemaphoreType.DMA((4,)),
        ],
        name="pack",
    )(queries, keys, values, grad_out)
    own = exchange(packed)
    squares = lax.all_gather(squares, "section")
    inverse = lax.rsqrt(jnp.sum(squares, axis=0) / total_width + norm_eps)
    inverse = jnp.broadcast_to(inverse, (seq, 8, rows))
    own, inverse = lax.optimization_barrier((own, inverse))
    other = swap(own)
    inverse = lax.all_to_all(inverse, "seq", 0, 0, tiled=True)

    window = (chips + 1) * BLOCK
    own_out, other_out, sums = pl.pallas_call(
        functools.partial(attention_kernel, seq),
        out_shape=(chunk, chunk, jax.ShapeDtypeStruct((seq, 8, HEAD_DIM), jnp.float32)),
        in_specs=[SMEM] + [VMEM] * 5,
        out_specs=[VMEM] * 3,
        scratch_shapes=[
            pltpu.VMEM((4, window, HEAD_DIM), jnp.bfloat16),
            pltpu.VMEM((window, HEAD_DIM), jnp.float32),
            pltpu.VMEM((window, HEAD_DIM), jnp.float32),
            pltpu.VMEM((4, window, HEAD_DIM), jnp.bfloat16),
        ],
        compiler_params=pltpu.CompilerParams(vmem_limit_bytes=40 * 2**20),
        cost_estimate=pl.CostEstimate(
            flops=12 * window * window * HEAD_DIM,
            transcendentals=window * window,
            bytes_accessed=16 * chips * rows * HEAD_DIM * 2,
        ),
        name="attention",
    )(lengths, own, other, inverse, query_gain, key_gain)

    other_out = swap(other_out)
    sums = lax.all_to_all(sums, "seq", 0, 0, tiled=True)
    sums, other_out = lax.optimization_barrier((sums, other_out))
    back = exchange(own_out + other_out)
    sums = jnp.sum(sums[: 2 * heads, 0:4].reshape(heads, 2, 4, HEAD_DIM), axis=1)
    inner = lax.all_gather(jnp.sum(sums[:, 0:2], axis=0), "section")
    gains = lax.psum((sums[:, 2] / query_gain, sums[:, 3] / key_gain), "dp")

    whole = jax.ShapeDtypeStruct((1, rows, width), jnp.bfloat16)
    grads = pl.pallas_call(
        functools.partial(final_kernel, total_width),
        out_shape=(whole, whole, whole, whole),
        in_specs=[VMEM] * 7,
        out_specs=[VMEM] * 4,
        compiler_params=pltpu.CompilerParams(vmem_limit_bytes=12 * 2**20),
        name="final",
    )(queries, keys, squares, query_gain, key_gain, inner, back)
    return (*grads, gains[0].reshape(width), gains[1].reshape(width))


def solution(mesh):
    rows = P("dp", "seq", "section")
    features = P("section")
    return jax.shard_map(
        local,
        mesh=mesh,
        in_specs=(rows, rows, rows, rows, P("dp", None), features, features),
        out_specs=(rows, rows, rows, rows, features, features),
        check_vma=False,
    )
```

```python
import functools
import math

import jax
import jax.numpy as jnp
from jax import lax
from jax.experimental import pallas as pl
from jax.experimental.pallas import tpu as pltpu
from jax.sharding import PartitionSpec as P

HEAD_DIM = 128
BLOCK = 128
norm_eps = 1e-06
masked_score = -1e30

VMEM = pl.BlockSpec(memory_space=pltpu.VMEM)
SMEM = pl.BlockSpec(memory_space=pltpu.SMEM)


def as_row(column):
    return jnp.broadcast_to(column, (BLOCK, BLOCK)).T[0:1]


def as_column(row):
    return jnp.broadcast_to(row, (BLOCK, BLOCK)).T[:, 0:1]


def inverses(squares, total_width):
    summed = jnp.sum(squares[...], axis=0)
    inverse = lax.rsqrt(summed / total_width + norm_eps)
    return as_column(inverse[0:1]), as_column(inverse[1:2])


def pack_kernel(queries, keys, values, grad_out, out, squares, held, buffer, in_sems, out_sems):
    heads = buffer.shape[0]
    refs = (queries, keys, values, grad_out)
    arrive = [pltpu.make_async_copy(ref, held.at[t], in_sems.at[t]) for t, ref in enumerate(refs)]
    for copy in arrive:
        copy.start()
    leave = []
    for t in range(4):
        arrive[t].wait()
        lines = pl.ds(t * BLOCK, BLOCK)
        for h in range(heads):
            buffer[h, lines, :] = held[t, 0, :, h * HEAD_DIM : (h + 1) * HEAD_DIM]
        place = out.at[pl.ds(0, heads), lines, :]
        leave.append(pltpu.make_async_copy(buffer.at[:, lines, :], place, out_sems.at[t]))
        leave[t].start()
    squares[...] = jnp.zeros_like(squares)
    for t in range(2):
        floats = held[t, 0].astype(jnp.float32)
        squares[t : t + 1, :] = as_row(jnp.sum(floats * floats, axis=1, keepdims=True))
    for copy in leave:
        copy.wait()


def halves(floats):
    high = floats.astype(jnp.bfloat16).astype(jnp.float32)
    return [high, floats - high]


def attention_kernel(
    blocks,
    lengths,
    own,
    other,
    inverse,
    query_gain,
    key_gain,
    own_out,
    other_out,
    sums,
    win,
    kacc,
    vacc,
    res,
):
    span = win.shape[1] // BLOCK
    width = span * BLOCK
    total = blocks * BLOCK
    scale = 1.0 / math.sqrt(HEAD_DIM)
    core = lax.rem(lax.axis_index("seq"), 2)
    head = jnp.minimum(lax.div(lax.axis_index("seq"), 2), query_gain.shape[0] - 1)
    ends = [lengths[0, 0]]
    long_clip = jnp.int32(0)
    begin = jnp.int32(0)
    for c in range(1, 4):
        is_long = lengths[0, c] == total // 2
        long_clip = jnp.where(is_long, c, long_clip)
        begin = jnp.where(is_long, ends[-1], begin)
        ends.append(ends[-1] + lengths[0, c])
    first = lax.rem(lax.div(begin, BLOCK) + core * (blocks // 2), blocks)

    def place(j):
        block = lax.rem(first + j, blocks)
        return block, lax.div(block, 2), lax.rem(block, 2) == core

    fold = scale * math.log2(math.e)
    gains = (query_gain[pl.ds(head, 1), :] * fold, key_gain[pl.ds(head, 1), :])
    for j in range(span):
        block, at, mine = place(j)
        for t in range(4):
            part = slice(t * BLOCK, (t + 1) * BLOCK)
            rows = jnp.where(mine, own[at, part, :], other[at, part, :])
            if t < 2:
                rows = rows.astype(jnp.float32) * as_column(inverse[block, t : t + 1, :]) * gains[t]
            win[t, j * BLOCK : (j + 1) * BLOCK, :] = rows.astype(jnp.bfloat16)

    def clip_of(offset, shape, axis):
        token = lax.rem(first * BLOCK + offset + lax.broadcasted_iota(jnp.int32, shape, axis), total)
        clip = jnp.zeros(shape, jnp.int32)
        for end in ends:
            clip = clip + (token >= end).astype(jnp.int32)
        return clip, (clip == long_clip) == (core == 0)

    key_clip, key_valid = clip_of(0, (1, width), 1)
    key_clip = jnp.where(key_valid, key_clip, -1)
    keys = win[1]
    values = win[2]
    sums[...] = jnp.zeros_like(sums)
    query_total = jnp.zeros((1, HEAD_DIM), jnp.float32)

    nt = (((1,), (1,)), ((), ()))
    tn = (((0,), (0,)), ((), ()))
    ones = jnp.ones((8, HEAD_DIM), jnp.bfloat16)

    def row_sums(products):
        return sum(
            lax.dot_general(ones, part.astype(jnp.bfloat16), nt, preferred_element_type=jnp.float32)[0:1]
            for part in halves(products)
        )

    def put_sums(start, t, products):
        row = row_sums(products)
        for r in range(products.shape[0] // BLOCK):
            block = lax.rem(first + start // BLOCK + r, blocks)
            sums[block, t : t + 1, :] = row[:, r * BLOCK : (r + 1) * BLOCK]

    bounds = (0, span // 2, span)
    parts = [slice(b * BLOCK, e * BLOCK) for b, e in zip(bounds, bounds[1:])]

    def start(part):
        return lax.dot_general(win[0, part, :], keys, nt, preferred_element_type=jnp.float32)

    raw = start(parts[0])
    for i, part in enumerate(parts):
        query = win[0, part, :]
        grad = win[3, part, :].astype(jnp.float32)
        row_clip, row_valid = clip_of(part.start, (part.stop - part.start, 1), 0)
        row_clip = jnp.where(row_valid, row_clip, -2)
        scores = jnp.where(row_clip == key_clip, raw, masked_score)
        row_max = jnp.max(scores, axis=1, keepdims=True)
        if i + 1 < len(parts):
            raw = start(parts[i + 1])
        weights = jnp.exp2(scores - row_max)
        row_total = jnp.sum(weights, axis=1, keepdims=True)
        row_inv = jnp.where(row_valid, 1.0 / row_total, 0.0)
        low = weights.astype(jnp.bfloat16)
        attended = (jnp.dot(low, values, preferred_element_type=jnp.float32) * row_inv).astype(jnp.bfloat16)
        grad = grad * row_inv
        delta = jnp.sum(grad * attended.astype(jnp.float32), axis=1, keepdims=True)
        grad = grad.astype(jnp.bfloat16)
        dots = lax.dot_general(grad, values, nt, preferred_element_type=jnp.float32)
        grad_scores = (weights * (dots - delta)).astype(jnp.bfloat16)
        query_norm_grad = jnp.dot(grad_scores, keys, preferred_element_type=jnp.float32) * scale
        value_part = lax.dot_general(low, grad, tn, preferred_element_type=jnp.float32)
        key_part = lax.dot_general(grad_scores, query, tn, preferred_element_type=jnp.float32)
        if i == 0:
            vacc[...] = value_part
            kacc[...] = key_part
        else:
            vacc[...] += value_part
            kacc[...] += key_part
        products = query_norm_grad * (query.astype(jnp.float32) * (1.0 / fold))
        query_total = query_total + jnp.sum(products, axis=0, keepdims=True)
        put_sums(part.start, 0, products)
        res[0, part, :] = query_norm_grad.astype(jnp.bfloat16)
        res[2, part, :] = attended
    key_norm_grad = kacc[...] * (scale / fold)
    products = key_norm_grad * keys.astype(jnp.float32)
    key_total = jnp.sum(products, axis=0, keepdims=True)
    put_sums(0, 1, products)
    res[1] = key_norm_grad.astype(jnp.bfloat16)
    res[3] = vacc[...].astype(jnp.bfloat16)

    for j in range(blocks):
        _, at, mine = place(j)

        def store(out, at=at, j=j):
            if j >= span:
                out[at] = jnp.zeros(out.shape[1:], out.dtype)
                return
            for t in range(4):
                out[at, t * BLOCK : (t + 1) * BLOCK, :] = res[t, j * BLOCK : (j + 1) * BLOCK, :]

        pl.when(mine)(functools.partial(store, own_out))
        pl.when(jnp.logical_not(mine))(functools.partial(store, other_out))

    for block in range(blocks):
        sums[block, 2:3, :] = query_total
        sums[block, 3:4, :] = key_total


def final_kernel(
    total_width,
    queries,
    keys,
    squares,
    query_gain,
    key_gain,
    inner,
    back,
    attended,
    query_grad,
    key_grad,
    value_grad,
):
    heads = query_gain.shape[0]
    invs, factors = [], []
    lines = jnp.sum(inner[...], axis=0)
    for t, inverse in enumerate(inverses(squares, total_width)):
        invs.append(jnp.broadcast_to(inverse, (BLOCK, HEAD_DIM)))
        factor = inverse * inverse * as_column(lines[t : t + 1]) / total_width
        factors.append(jnp.broadcast_to(factor, (BLOCK, HEAD_DIM)))
    for h in range(heads):
        cols = slice(h * HEAD_DIM, (h + 1) * HEAD_DIM)
        for t, (ref, gain, grad) in enumerate(((queries, query_gain, query_grad), (keys, key_gain, key_grad))):
            norm_grad = back[h, t * BLOCK : (t + 1) * BLOCK, :].astype(jnp.float32)
            scaled = invs[t] * gain[h : h + 1, :] * norm_grad
            grad[0, :, cols] = (scaled - ref[0, :, cols].astype(jnp.float32) * factors[t]).astype(jnp.bfloat16)
        attended[0, :, cols] = back[h, 2 * BLOCK : 3 * BLOCK, :]
        value_grad[0, :, cols] = back[h, 3 * BLOCK : 4 * BLOCK, :]


def local(queries, keys, values, grad_out, lengths, query_gain, key_gain):
    rows, width = queries.shape[1:]
    heads = width // HEAD_DIM
    total_width = width * lax.axis_size("section")
    seq = lax.axis_size("seq")
    chips = seq // 2
    same_core = [[2 * z + c for z in range(chips)] for c in range(2)]
    other_core = [(i, i ^ 1) for i in range(seq)]
    query_gain, key_gain = query_gain.reshape(heads, HEAD_DIM), key_gain.reshape(heads, HEAD_DIM)
    chunk = jax.ShapeDtypeStruct((chips, 4 * rows, HEAD_DIM), jnp.bfloat16)

    def exchange(chunks):
        return lax.all_to_all(chunks, "seq", 0, 0, axis_index_groups=same_core, tiled=True)

    def swap(array):
        return lax.ppermute(array, "seq", other_core)

    hbm = pl.BlockSpec(memory_space=pl.ANY)
    packed, squares = pl.pallas_call(
        pack_kernel,
        out_shape=(chunk, jax.ShapeDtypeStruct((8, rows), jnp.float32)),
        in_specs=[hbm] * 4,
        out_specs=(hbm, VMEM),
        scratch_shapes=[
            pltpu.VMEM((4, 1, rows, width), jnp.bfloat16),
            pltpu.VMEM((heads, 4 * rows, HEAD_DIM), jnp.bfloat16),
            pltpu.SemaphoreType.DMA((4,)),
            pltpu.SemaphoreType.DMA((4,)),
        ],
        name="pack",
    )(queries, keys, values, grad_out)
    own = exchange(packed)
    squares = lax.all_gather(squares, "section")
    inverse = lax.rsqrt(jnp.sum(squares, axis=0) / total_width + norm_eps)
    inverse = lax.all_gather(inverse[0:2], "seq")
    own, inverse = lax.optimization_barrier((own, inverse))
    other = swap(own)

    window = (chips + 1) * BLOCK
    own_out, other_out, sums = pl.pallas_call(
        functools.partial(attention_kernel, seq),
        out_shape=(chunk, chunk, jax.ShapeDtypeStruct((seq, 8, HEAD_DIM), jnp.float32)),
        in_specs=[SMEM] + [VMEM] * 5,
        out_specs=[VMEM] * 3,
        scratch_shapes=[
            pltpu.VMEM((4, window, HEAD_DIM), jnp.bfloat16),
            pltpu.VMEM((window, HEAD_DIM), jnp.float32),
            pltpu.VMEM((window, HEAD_DIM), jnp.float32),
            pltpu.VMEM((4, window, HEAD_DIM), jnp.bfloat16),
        ],
        compiler_params=pltpu.CompilerParams(vmem_limit_bytes=40 * 2**20),
        cost_estimate=pl.CostEstimate(
            flops=12 * window * window * HEAD_DIM,
            transcendentals=window * window,
            bytes_accessed=16 * chips * rows * HEAD_DIM * 2,
        ),
        name="attention",
    )(lengths, own, other, inverse, query_gain, key_gain)

    other_out = swap(other_out)
    sums = lax.all_to_all(sums, "seq", 0, 0, tiled=True)
    sums, other_out = lax.optimization_barrier((sums, other_out))
    back = exchange(own_out + other_out)
    sums = jnp.sum(sums[: 2 * heads, 0:4].reshape(heads, 2, 4, HEAD_DIM), axis=1)
    inner = lax.all_gather(jnp.sum(sums[:, 0:2], axis=0), "section")
    gains = lax.psum((sums[:, 2] / query_gain, sums[:, 3] / key_gain), "dp")

    whole = jax.ShapeDtypeStruct((1, rows, width), jnp.bfloat16)
    grads = pl.pallas_call(
        functools.partial(final_kernel, total_width),
        out_shape=(whole, whole, whole, whole),
        in_specs=[VMEM] * 7,
        out_specs=[VMEM] * 4,
        compiler_params=pltpu.CompilerParams(vmem_limit_bytes=12 * 2**20),
        name="final",
    )(queries, keys, squares, query_gain, key_gain, inner, back)
    return (*grads, gains[0].reshape(width), gains[1].reshape(width))


def solution(mesh):
    rows = P("dp", "seq", "section")
    features = P("section")
    return jax.shard_map(
        local,
        mesh=mesh,
        in_specs=(rows, rows, rows, rows, P("dp", None), features, features),
        out_specs=(rows, rows, rows, rows, features, features),
        check_vma=False,
    )
```

```python
import functools
import math

import jax
import jax.numpy as jnp
from jax import lax
from jax.experimental import pallas as pl
from jax.experimental.pallas import tpu as pltpu
from jax.sharding import PartitionSpec as P

HEAD_DIM = 128
BLOCK = 128
norm_eps = 1e-06
masked_score = -1e30

VMEM = pl.BlockSpec(memory_space=pltpu.VMEM)
SMEM = pl.BlockSpec(memory_space=pltpu.SMEM)


def as_row(column):
    return jnp.broadcast_to(column, (BLOCK, BLOCK)).T[0:1]


def as_column(row):
    return jnp.broadcast_to(row, (BLOCK, BLOCK)).T[:, 0:1]


def pack_kernel(queries, keys, values, grad_out, out, squares, held, buffer, in_sems, out_sems):
    heads = buffer.shape[0]
    refs = (queries, keys, values, grad_out)
    arrive = [pltpu.make_async_copy(ref, held.at[t], in_sems.at[t]) for t, ref in enumerate(refs)]
    for copy in arrive:
        copy.start()
    leave = []
    for t in range(4):
        arrive[t].wait()
        lines = pl.ds(t * BLOCK, BLOCK)
        for h in range(heads):
            buffer[h, lines, :] = held[t, 0, :, h * HEAD_DIM : (h + 1) * HEAD_DIM]
        place = out.at[pl.ds(0, heads), lines, :]
        leave.append(pltpu.make_async_copy(buffer.at[:, lines, :], place, out_sems.at[t]))
        leave[t].start()
    for t in range(2):
        floats = held[t, 0].astype(jnp.float32)
        squares[t : t + 1, :] = as_row(jnp.sum(floats * floats, axis=1, keepdims=True))
    for copy in leave:
        copy.wait()


def halves(floats):
    high = floats.astype(jnp.bfloat16).astype(jnp.float32)
    return [high, floats - high]


def attention_kernel(
    blocks,
    lengths,
    own,
    other,
    inverse,
    query_gain,
    key_gain,
    own_out,
    other_out,
    sums,
    win,
    kacc,
    vacc,
    res,
):
    span = win.shape[1] // BLOCK
    width = span * BLOCK
    total = blocks * BLOCK
    scale = 1.0 / math.sqrt(HEAD_DIM)
    core = lax.rem(lax.axis_index("seq"), 2)
    head = jnp.minimum(lax.div(lax.axis_index("seq"), 2), query_gain.shape[0] - 1)
    ends = [lengths[0, 0]]
    long_clip = jnp.int32(0)
    begin = jnp.int32(0)
    for c in range(1, 4):
        is_long = lengths[0, c] == total // 2
        long_clip = jnp.where(is_long, c, long_clip)
        begin = jnp.where(is_long, ends[-1], begin)
        ends.append(ends[-1] + lengths[0, c])
    first = lax.rem(lax.div(begin, BLOCK) + core * (blocks // 2), blocks)

    def place(j):
        block = lax.rem(first + j, blocks)
        return block, lax.div(block, 2), lax.rem(block, 2) == core

    fold = scale * math.log2(math.e)
    gains = (query_gain[pl.ds(head, 1), :] * fold, key_gain[pl.ds(head, 1), :])
    for j in range(span):
        block, at, mine = place(j)
        for t in range(4):
            part = slice(t * BLOCK, (t + 1) * BLOCK)
            rows = jnp.where(mine, own[at, part, :], other[at, part, :])
            if t < 2:
                rows = rows.astype(jnp.float32) * as_column(inverse[block, t : t + 1, :]) * gains[t]
            win[t, j * BLOCK : (j + 1) * BLOCK, :] = rows.astype(jnp.bfloat16)

    def clip_of(offset, shape, axis):
        token = lax.rem(first * BLOCK + offset + lax.broadcasted_iota(jnp.int32, shape, axis), total)
        clip = jnp.zeros(shape, jnp.int32)
        for end in ends:
            clip = clip + (token >= end).astype(jnp.int32)
        return clip, (clip == long_clip) == (core == 0)

    key_clip, key_valid = clip_of(0, (1, width), 1)
    key_clip = jnp.where(key_valid, key_clip, -1)
    keys = win[1]
    values = win[2]
    sums[...] = jnp.zeros_like(sums)
    query_total = jnp.zeros((1, HEAD_DIM), jnp.float32)

    nt = (((1,), (1,)), ((), ()))
    tn = (((0,), (0,)), ((), ()))
    ones = jnp.ones((8, HEAD_DIM), jnp.bfloat16)

    def row_sums(products):
        return sum(
            lax.dot_general(ones, part.astype(jnp.bfloat16), nt, preferred_element_type=jnp.float32)[0:1]
            for part in halves(products)
        )

    def put_sums(start, t, products):
        row = row_sums(products)
        for r in range(products.shape[0] // BLOCK):
            block = lax.rem(first + start // BLOCK + r, blocks)
            sums[block, t : t + 1, :] = row[:, r * BLOCK : (r + 1) * BLOCK]

    bounds = (0, span // 2, span)
    parts = [slice(b * BLOCK, e * BLOCK) for b, e in zip(bounds, bounds[1:])]

    def start(part):
        return lax.dot_general(win[0, part, :], keys, nt, preferred_element_type=jnp.float32)

    raw = start(parts[0])
    for i, part in enumerate(parts):
        query = win[0, part, :]
        grad = win[3, part, :].astype(jnp.float32)
        row_clip, row_valid = clip_of(part.start, (part.stop - part.start, 1), 0)
        row_clip = jnp.where(row_valid, row_clip, -2)
        scores = jnp.where(row_clip == key_clip, raw, masked_score)
        row_max = jnp.max(scores, axis=1, keepdims=True)
        if i + 1 < len(parts):
            raw = start(parts[i + 1])
        weights = jnp.exp2(scores - row_max)
        row_total = jnp.sum(weights, axis=1, keepdims=True)
        row_inv = jnp.where(row_valid, 1.0 / row_total, 0.0)
        low = weights.astype(jnp.bfloat16)
        attended = (jnp.dot(low, values, preferred_element_type=jnp.float32) * row_inv).astype(jnp.bfloat16)
        grad = grad * row_inv
        delta = jnp.sum(grad * attended.astype(jnp.float32), axis=1, keepdims=True)
        grad = grad.astype(jnp.bfloat16)
        dots = lax.dot_general(grad, values, nt, preferred_element_type=jnp.float32)
        grad_scores = (weights * (dots - delta)).astype(jnp.bfloat16)
        query_norm_grad = jnp.dot(grad_scores, keys, preferred_element_type=jnp.float32) * scale
        value_part = lax.dot_general(low, grad, tn, preferred_element_type=jnp.float32)
        key_part = lax.dot_general(grad_scores, query, tn, preferred_element_type=jnp.float32)
        if i == 0:
            vacc[...] = value_part
            kacc[...] = key_part
        else:
            vacc[...] += value_part
            kacc[...] += key_part
        products = query_norm_grad * (query.astype(jnp.float32) * (1.0 / fold))
        query_total = query_total + jnp.sum(products, axis=0, keepdims=True)
        put_sums(part.start, 0, products)
        res[0, part, :] = query_norm_grad.astype(jnp.bfloat16)
        res[2, part, :] = attended
    key_norm_grad = kacc[...] * (scale / fold)
    products = key_norm_grad * keys.astype(jnp.float32)
    key_total = jnp.sum(products, axis=0, keepdims=True)
    put_sums(0, 1, products)
    res[1] = key_norm_grad.astype(jnp.bfloat16)
    res[3] = vacc[...].astype(jnp.bfloat16)

    for j in range(blocks):
        _, at, mine = place(j)

        def store(out, at=at, j=j):
            if j >= span:
                out[at] = jnp.zeros(out.shape[1:], out.dtype)
                return
            for t in range(4):
                out[at, t * BLOCK : (t + 1) * BLOCK, :] = res[t, j * BLOCK : (j + 1) * BLOCK, :]

        pl.when(mine)(functools.partial(store, own_out))
        pl.when(jnp.logical_not(mine))(functools.partial(store, other_out))

    for block in range(blocks):
        sums[block, 2:3, :] = query_total
        sums[block, 3:4, :] = key_total


def final_kernel(
    total_width,
    queries,
    keys,
    inverse,
    query_gain,
    key_gain,
    inner,
    back,
    attended,
    query_grad,
    key_grad,
    value_grad,
):
    heads = query_gain.shape[0]
    invs, factors = [], []
    lines = jnp.sum(inner[...], axis=0)
    for t in range(2):
        column = as_column(inverse[lax.axis_index("seq"), t : t + 1, :])
        invs.append(jnp.broadcast_to(column, (BLOCK, HEAD_DIM)))
        factor = column * column * as_column(lines[t : t + 1]) / total_width
        factors.append(jnp.broadcast_to(factor, (BLOCK, HEAD_DIM)))
    for h in range(heads):
        cols = slice(h * HEAD_DIM, (h + 1) * HEAD_DIM)
        for t, (ref, gain, grad) in enumerate(((queries, query_gain, query_grad), (keys, key_gain, key_grad))):
            norm_grad = back[h, t * BLOCK : (t + 1) * BLOCK, :].astype(jnp.float32)
            scaled = invs[t] * gain[h : h + 1, :] * norm_grad
            grad[0, :, cols] = (scaled - ref[0, :, cols].astype(jnp.float32) * factors[t]).astype(jnp.bfloat16)
        attended[0, :, cols] = back[h, 2 * BLOCK : 3 * BLOCK, :]
        value_grad[0, :, cols] = back[h, 3 * BLOCK : 4 * BLOCK, :]


def local(queries, keys, values, grad_out, lengths, query_gain, key_gain):
    rows, width = queries.shape[1:]
    heads = width // HEAD_DIM
    total_width = width * lax.axis_size("section")
    seq = lax.axis_size("seq")
    chips = seq // 2
    same_core = [[2 * z + c for z in range(chips)] for c in range(2)]
    other_core = [(i, i ^ 1) for i in range(seq)]
    query_gain, key_gain = query_gain.reshape(heads, HEAD_DIM), key_gain.reshape(heads, HEAD_DIM)
    chunk = jax.ShapeDtypeStruct((chips, 4 * rows, HEAD_DIM), jnp.bfloat16)

    def exchange(chunks):
        return lax.all_to_all(chunks, "seq", 0, 0, axis_index_groups=same_core, tiled=True)

    def swap(array):
        return lax.ppermute(array, "seq", other_core)

    hbm = pl.BlockSpec(memory_space=pl.ANY)
    packed, squares = pl.pallas_call(
        pack_kernel,
        out_shape=(chunk, jax.ShapeDtypeStruct((2, rows), jnp.float32)),
        in_specs=[hbm] * 4,
        out_specs=(hbm, VMEM),
        scratch_shapes=[
            pltpu.VMEM((4, 1, rows, width), jnp.bfloat16),
            pltpu.VMEM((heads, 4 * rows, HEAD_DIM), jnp.bfloat16),
            pltpu.SemaphoreType.DMA((4,)),
            pltpu.SemaphoreType.DMA((4,)),
        ],
        name="pack",
    )(queries, keys, values, grad_out)
    own = exchange(packed)
    squares = lax.all_gather(lax.all_gather(squares, "seq"), "section")
    inverse = lax.rsqrt(jnp.sum(squares, axis=0) / total_width + norm_eps)
    own, inverse = lax.optimization_barrier((own, inverse))
    other = swap(own)

    window = (chips + 1) * BLOCK
    own_out, other_out, sums = pl.pallas_call(
        functools.partial(attention_kernel, seq),
        out_shape=(chunk, chunk, jax.ShapeDtypeStruct((seq, 8, HEAD_DIM), jnp.float32)),
        in_specs=[SMEM] + [VMEM] * 5,
        out_specs=[VMEM] * 3,
        scratch_shapes=[
            pltpu.VMEM((4, window, HEAD_DIM), jnp.bfloat16),
            pltpu.VMEM((window, HEAD_DIM), jnp.float32),
            pltpu.VMEM((window, HEAD_DIM), jnp.float32),
            pltpu.VMEM((4, window, HEAD_DIM), jnp.bfloat16),
        ],
        compiler_params=pltpu.CompilerParams(vmem_limit_bytes=40 * 2**20),
        cost_estimate=pl.CostEstimate(
            flops=12 * window * window * HEAD_DIM,
            transcendentals=window * window,
            bytes_accessed=16 * chips * rows * HEAD_DIM * 2,
        ),
        name="attention",
    )(lengths, own, other, inverse, query_gain, key_gain)

    other_out = swap(other_out)
    sums = lax.all_to_all(sums, "seq", 0, 0, tiled=True)
    sums, other_out = lax.optimization_barrier((sums, other_out))
    back = exchange(own_out + other_out)
    sums = jnp.sum(sums[: 2 * heads, 0:4].reshape(heads, 2, 4, HEAD_DIM), axis=1)
    inner = lax.all_gather(jnp.sum(sums[:, 0:2], axis=0), "section")
    gains = lax.psum((sums[:, 2] / query_gain, sums[:, 3] / key_gain), "dp")

    whole = jax.ShapeDtypeStruct((1, rows, width), jnp.bfloat16)
    grads = pl.pallas_call(
        functools.partial(final_kernel, total_width),
        out_shape=(whole, whole, whole, whole),
        in_specs=[VMEM] * 7,
        out_specs=[VMEM] * 4,
        compiler_params=pltpu.CompilerParams(vmem_limit_bytes=12 * 2**20),
        name="final",
    )(queries, keys, inverse, query_gain, key_gain, inner, back)
    return (*grads, gains[0].reshape(width), gains[1].reshape(width))


def solution(mesh):
    rows = P("dp", "seq", "section")
    features = P("section")
    return jax.shard_map(
        local,
        mesh=mesh,
        in_specs=(rows, rows, rows, rows, P("dp", None), features, features),
        out_specs=(rows, rows, rows, rows, features, features),
        check_vma=False,
    )
```

```python
import functools
import math

import jax
import jax.numpy as jnp
from jax import lax
from jax.experimental import pallas as pl
from jax.experimental.pallas import tpu as pltpu
from jax.sharding import PartitionSpec as P

HEAD_DIM = 128
BLOCK = 128
norm_eps = 1e-06
masked_score = -1e30

VMEM = pl.BlockSpec(memory_space=pltpu.VMEM)
SMEM = pl.BlockSpec(memory_space=pltpu.SMEM)


def as_row(column):
    return jnp.broadcast_to(column, (BLOCK, BLOCK)).T[0:1]


def as_column(row):
    return jnp.broadcast_to(row, (BLOCK, BLOCK)).T[:, 0:1]


def inverses(squares, total_width):
    summed = jnp.sum(squares[...], axis=0)
    inverse = lax.rsqrt(summed / total_width + norm_eps)
    return as_column(inverse[0:1]), as_column(inverse[1:2])


def squares_kernel(queries, keys, out):
    out[...] = jnp.zeros_like(out)
    for t, ref in enumerate((queries, keys)):
        floats = ref[0].astype(jnp.float32)
        out[t : t + 1, :] = as_row(jnp.sum(floats * floats, axis=1, keepdims=True))


def pack_kernel(queries, keys, values, grad_out, out, held, buffer, in_sems, out_sems):
    heads = buffer.shape[0]
    refs = (queries, keys, values, grad_out)
    arrive = [pltpu.make_async_copy(ref, held.at[t], in_sems.at[t]) for t, ref in enumerate(refs)]
    for copy in arrive:
        copy.start()
    leave = []
    for t in range(4):
        arrive[t].wait()
        lines = pl.ds(t * BLOCK, BLOCK)
        for h in range(heads):
            buffer[h, lines, :] = held[t, 0, :, h * HEAD_DIM : (h + 1) * HEAD_DIM]
        place = out.at[pl.ds(0, heads), lines, :]
        leave.append(pltpu.make_async_copy(buffer.at[:, lines, :], place, out_sems.at[t]))
        leave[t].start()
    for copy in leave:
        copy.wait()


def halves(floats):
    high = floats.astype(jnp.bfloat16).astype(jnp.float32)
    return [high, floats - high]


def attention_kernel(
    blocks,
    lengths,
    own,
    other,
    inverse,
    query_gain,
    key_gain,
    own_out,
    other_out,
    sums,
    win,
    kacc,
    vacc,
    res,
):
    span = win.shape[1] // BLOCK
    width = span * BLOCK
    total = blocks * BLOCK
    scale = 1.0 / math.sqrt(HEAD_DIM)
    core = lax.rem(lax.axis_index("seq"), 2)
    head = jnp.minimum(lax.div(lax.axis_index("seq"), 2), query_gain.shape[0] - 1)
    ends = [lengths[0, 0]]
    long_clip = jnp.int32(0)
    begin = jnp.int32(0)
    for c in range(1, 4):
        is_long = lengths[0, c] == total // 2
        long_clip = jnp.where(is_long, c, long_clip)
        begin = jnp.where(is_long, ends[-1], begin)
        ends.append(ends[-1] + lengths[0, c])
    first = lax.rem(lax.div(begin, BLOCK) + core * (blocks // 2), blocks)

    def place(j):
        block = lax.rem(first + j, blocks)
        return block, lax.div(block, 2), lax.rem(block, 2) == core

    fold = scale * math.log2(math.e)
    gains = (query_gain[pl.ds(head, 1), :] * fold, key_gain[pl.ds(head, 1), :])
    for j in range(span):
        block, at, mine = place(j)
        for t in range(4):
            part = slice(t * BLOCK, (t + 1) * BLOCK)
            rows = jnp.where(mine, own[at, part, :], other[at, part, :])
            if t < 2:
                rows = rows.astype(jnp.float32) * as_column(inverse[block, t : t + 1, :]) * gains[t]
            win[t, j * BLOCK : (j + 1) * BLOCK, :] = rows.astype(jnp.bfloat16)

    def clip_of(offset, shape, axis):
        token = lax.rem(first * BLOCK + offset + lax.broadcasted_iota(jnp.int32, shape, axis), total)
        clip = jnp.zeros(shape, jnp.int32)
        for end in ends:
            clip = clip + (token >= end).astype(jnp.int32)
        return clip, (clip == long_clip) == (core == 0)

    key_clip, key_valid = clip_of(0, (1, width), 1)
    key_clip = jnp.where(key_valid, key_clip, -1)
    keys = win[1]
    values = win[2]
    sums[...] = jnp.zeros_like(sums)
    query_total = jnp.zeros((1, HEAD_DIM), jnp.float32)

    nt = (((1,), (1,)), ((), ()))
    tn = (((0,), (0,)), ((), ()))
    ones = jnp.ones((8, HEAD_DIM), jnp.bfloat16)

    def row_sums(products):
        return sum(
            lax.dot_general(ones, part.astype(jnp.bfloat16), nt, preferred_element_type=jnp.float32)[0:1]
            for part in halves(products)
        )

    def put_sums(start, t, products):
        row = row_sums(products)
        for r in range(products.shape[0] // BLOCK):
            block = lax.rem(first + start // BLOCK + r, blocks)
            sums[block, t : t + 1, :] = row[:, r * BLOCK : (r + 1) * BLOCK]

    bounds = (0, span // 2, span)
    parts = [slice(b * BLOCK, e * BLOCK) for b, e in zip(bounds, bounds[1:])]

    def start(part):
        return lax.dot_general(win[0, part, :], keys, nt, preferred_element_type=jnp.float32)

    raw = start(parts[0])
    for i, part in enumerate(parts):
        query = win[0, part, :]
        grad = win[3, part, :].astype(jnp.float32)
        row_clip, row_valid = clip_of(part.start, (part.stop - part.start, 1), 0)
        row_clip = jnp.where(row_valid, row_clip, -2)
        scores = jnp.where(row_clip == key_clip, raw, masked_score)
        row_max = jnp.max(scores, axis=1, keepdims=True)
        if i + 1 < len(parts):
            raw = start(parts[i + 1])
        weights = jnp.exp2(scores - row_max)
        row_total = jnp.sum(weights, axis=1, keepdims=True)
        row_inv = jnp.where(row_valid, 1.0 / row_total, 0.0)
        low = weights.astype(jnp.bfloat16)
        attended = (jnp.dot(low, values, preferred_element_type=jnp.float32) * row_inv).astype(jnp.bfloat16)
        grad = grad * row_inv
        delta = jnp.sum(grad * attended.astype(jnp.float32), axis=1, keepdims=True)
        grad = grad.astype(jnp.bfloat16)
        dots = lax.dot_general(grad, values, nt, preferred_element_type=jnp.float32)
        grad_scores = (weights * (dots - delta)).astype(jnp.bfloat16)
        query_norm_grad = jnp.dot(grad_scores, keys, preferred_element_type=jnp.float32) * scale
        value_part = lax.dot_general(low, grad, tn, preferred_element_type=jnp.float32)
        key_part = lax.dot_general(grad_scores, query, tn, preferred_element_type=jnp.float32)
        if i == 0:
            vacc[...] = value_part
            kacc[...] = key_part
        else:
            vacc[...] += value_part
            kacc[...] += key_part
        products = query_norm_grad * (query.astype(jnp.float32) * (1.0 / fold))
        query_total = query_total + jnp.sum(products, axis=0, keepdims=True)
        put_sums(part.start, 0, products)
        res[0, part, :] = query_norm_grad.astype(jnp.bfloat16)
        res[2, part, :] = attended
    key_norm_grad = kacc[...] * (scale / fold)
    products = key_norm_grad * keys.astype(jnp.float32)
    key_total = jnp.sum(products, axis=0, keepdims=True)
    put_sums(0, 1, products)
    res[1] = key_norm_grad.astype(jnp.bfloat16)
    res[3] = vacc[...].astype(jnp.bfloat16)

    for j in range(blocks):
        _, at, mine = place(j)

        def store(out, at=at, j=j):
            if j >= span:
                out[at] = jnp.zeros(out.shape[1:], out.dtype)
                return
            for t in range(4):
                out[at, t * BLOCK : (t + 1) * BLOCK, :] = res[t, j * BLOCK : (j + 1) * BLOCK, :]

        pl.when(mine)(functools.partial(store, own_out))
        pl.when(jnp.logical_not(mine))(functools.partial(store, other_out))

    for block in range(blocks):
        sums[block, 2:3, :] = query_total
        sums[block, 3:4, :] = key_total


def final_kernel(
    total_width,
    queries,
    keys,
    squares,
    query_gain,
    key_gain,
    inner,
    back,
    attended,
    query_grad,
    key_grad,
    value_grad,
):
    heads = query_gain.shape[0]
    invs, factors = [], []
    lines = jnp.sum(inner[...], axis=0)
    for t, inverse in enumerate(inverses(squares, total_width)):
        invs.append(jnp.broadcast_to(inverse, (BLOCK, HEAD_DIM)))
        factor = inverse * inverse * as_column(lines[t : t + 1]) / total_width
        factors.append(jnp.broadcast_to(factor, (BLOCK, HEAD_DIM)))
    for h in range(heads):
        cols = slice(h * HEAD_DIM, (h + 1) * HEAD_DIM)
        for t, (ref, gain, grad) in enumerate(((queries, query_gain, query_grad), (keys, key_gain, key_grad))):
            norm_grad = back[h, t * BLOCK : (t + 1) * BLOCK, :].astype(jnp.float32)
            scaled = invs[t] * gain[h : h + 1, :] * norm_grad
            grad[0, :, cols] = (scaled - ref[0, :, cols].astype(jnp.float32) * factors[t]).astype(jnp.bfloat16)
        attended[0, :, cols] = back[h, 2 * BLOCK : 3 * BLOCK, :]
        value_grad[0, :, cols] = back[h, 3 * BLOCK : 4 * BLOCK, :]


def local(queries, keys, values, grad_out, lengths, query_gain, key_gain):
    rows, width = queries.shape[1:]
    heads = width // HEAD_DIM
    total_width = width * lax.axis_size("section")
    seq = lax.axis_size("seq")
    chips = seq // 2
    same_core = [[2 * z + c for z in range(chips)] for c in range(2)]
    other_core = [(i, i ^ 1) for i in range(seq)]
    query_gain, key_gain = query_gain.reshape(heads, HEAD_DIM), key_gain.reshape(heads, HEAD_DIM)
    chunk = jax.ShapeDtypeStruct((chips, 4 * rows, HEAD_DIM), jnp.bfloat16)

    def exchange(chunks):
        return lax.all_to_all(chunks, "seq", 0, 0, axis_index_groups=same_core, tiled=True)

    def swap(array):
        return lax.ppermute(array, "seq", other_core)

    hbm = pl.BlockSpec(memory_space=pl.ANY)
    packed = pl.pallas_call(
        pack_kernel,
        out_shape=chunk,
        in_specs=[hbm] * 4,
        out_specs=hbm,
        scratch_shapes=[
            pltpu.VMEM((4, 1, rows, width), jnp.bfloat16),
            pltpu.VMEM((heads, 4 * rows, HEAD_DIM), jnp.bfloat16),
            pltpu.SemaphoreType.DMA((4,)),
            pltpu.SemaphoreType.DMA((4,)),
        ],
        name="pack",
    )(queries, keys, values, grad_out)
    own = exchange(packed)
    squares = pl.pallas_call(
        squares_kernel,
        out_shape=jax.ShapeDtypeStruct((8, rows), jnp.float32),
        in_specs=[VMEM] * 2,
        out_specs=VMEM,
        name="squares",
    )(queries, keys)
    squares = lax.all_gather(squares, "section")
    inverse = lax.rsqrt(jnp.sum(squares, axis=0) / total_width + norm_eps)
    inverse = jnp.broadcast_to(inverse, (seq, 8, rows))
    own, inverse = lax.optimization_barrier((own, inverse))
    other = swap(own)
    inverse = lax.all_to_all(inverse, "seq", 0, 0, tiled=True)

    window = (chips + 1) * BLOCK
    own_out, other_out, sums = pl.pallas_call(
        functools.partial(attention_kernel, seq),
        out_shape=(chunk, chunk, jax.ShapeDtypeStruct((seq, 8, HEAD_DIM), jnp.float32)),
        in_specs=[SMEM] + [VMEM] * 5,
        out_specs=[VMEM] * 3,
        scratch_shapes=[
            pltpu.VMEM((4, window, HEAD_DIM), jnp.bfloat16),
            pltpu.VMEM((window, HEAD_DIM), jnp.float32),
            pltpu.VMEM((window, HEAD_DIM), jnp.float32),
            pltpu.VMEM((4, window, HEAD_DIM), jnp.bfloat16),
        ],
        compiler_params=pltpu.CompilerParams(vmem_limit_bytes=40 * 2**20),
        cost_estimate=pl.CostEstimate(
            flops=12 * window * window * HEAD_DIM,
            transcendentals=window * window,
            bytes_accessed=16 * chips * rows * HEAD_DIM * 2,
        ),
        name="attention",
    )(lengths, own, other, inverse, query_gain, key_gain)

    merged = own_out + swap(other_out)
    sums = lax.all_to_all(sums, "seq", 0, 0, tiled=True)
    sums, merged = lax.optimization_barrier((sums, merged))
    back = exchange(merged)
    sums = jnp.sum(sums[: 2 * heads, 0:4].reshape(heads, 2, 4, HEAD_DIM), axis=1)
    inner = lax.all_gather(jnp.sum(sums[:, 0:2], axis=0), "section")
    gains = lax.psum((sums[:, 2] / query_gain, sums[:, 3] / key_gain), "dp")

    whole = jax.ShapeDtypeStruct((1, rows, width), jnp.bfloat16)
    grads = pl.pallas_call(
        functools.partial(final_kernel, total_width),
        out_shape=(whole, whole, whole, whole),
        in_specs=[VMEM] * 7,
        out_specs=[VMEM] * 4,
        compiler_params=pltpu.CompilerParams(vmem_limit_bytes=12 * 2**20),
        name="final",
    )(queries, keys, squares, query_gain, key_gain, inner, back)
    return (*grads, gains[0].reshape(width), gains[1].reshape(width))


def solution(mesh):
    rows = P("dp", "seq", "section")
    features = P("section")
    return jax.shard_map(
        local,
        mesh=mesh,
        in_specs=(rows, rows, rows, rows, P("dp", None), features, features),
        out_specs=(rows, rows, rows, rows, features, features),
        check_vma=False,
    )
```

```python
import functools
import math

import jax
import jax.numpy as jnp
from jax import lax
from jax.experimental import pallas as pl
from jax.experimental.pallas import tpu as pltpu
from jax.sharding import PartitionSpec as P

HEAD_DIM = 128
BLOCK = 128
norm_eps = 1e-06
masked_score = -1e30

VMEM = pl.BlockSpec(memory_space=pltpu.VMEM)
SMEM = pl.BlockSpec(memory_space=pltpu.SMEM)


def as_row(column):
    return jnp.broadcast_to(column, (BLOCK, BLOCK)).T[0:1]


def as_column(row):
    return jnp.broadcast_to(row, (BLOCK, BLOCK)).T[:, 0:1]


def inverses(squares, total_width):
    summed = jnp.sum(squares[...], axis=0)
    inverse = lax.rsqrt(summed / total_width + norm_eps)
    return as_column(inverse[0:1]), as_column(inverse[1:2])


def squares_kernel(queries, keys, out):
    for t, ref in enumerate((queries, keys)):
        floats = ref[0].astype(jnp.float32)
        out[t : t + 1, :] = as_row(jnp.sum(floats * floats, axis=1, keepdims=True))


def pack_kernel(queries, keys, values, grad_out, out, held, buffer, in_sems, out_sems):
    heads = buffer.shape[0]
    refs = (queries, keys, values, grad_out)
    arrive = [pltpu.make_async_copy(ref, held.at[t], in_sems.at[t]) for t, ref in enumerate(refs)]
    for copy in arrive:
        copy.start()
    leave = []
    for t in range(4):
        arrive[t].wait()
        lines = pl.ds(t * BLOCK, BLOCK)
        for h in range(heads):
            buffer[h, lines, :] = held[t, 0, :, h * HEAD_DIM : (h + 1) * HEAD_DIM]
        place = out.at[pl.ds(0, heads), lines, :]
        leave.append(pltpu.make_async_copy(buffer.at[:, lines, :], place, out_sems.at[t]))
        leave[t].start()
    for copy in leave:
        copy.wait()


def halves(floats):
    high = floats.astype(jnp.bfloat16).astype(jnp.float32)
    return [high, floats - high]


def attention_kernel(
    blocks,
    lengths,
    own,
    other,
    inverse,
    query_gain,
    key_gain,
    own_out,
    other_out,
    sums,
    win,
    kacc,
    vacc,
    res,
):
    span = win.shape[1] // BLOCK
    width = span * BLOCK
    total = blocks * BLOCK
    scale = 1.0 / math.sqrt(HEAD_DIM)
    core = lax.rem(lax.axis_index("seq"), 2)
    head = jnp.minimum(lax.div(lax.axis_index("seq"), 2), query_gain.shape[0] - 1)
    ends = [lengths[0, 0]]
    long_clip = jnp.int32(0)
    begin = jnp.int32(0)
    for c in range(1, 4):
        is_long = lengths[0, c] == total // 2
        long_clip = jnp.where(is_long, c, long_clip)
        begin = jnp.where(is_long, ends[-1], begin)
        ends.append(ends[-1] + lengths[0, c])
    first = lax.rem(lax.div(begin, BLOCK) + core * (blocks // 2), blocks)

    def place(j):
        block = lax.rem(first + j, blocks)
        return block, lax.div(block, 2), lax.rem(block, 2) == core

    fold = scale * math.log2(math.e)
    gains = (query_gain[pl.ds(head, 1), :] * fold, key_gain[pl.ds(head, 1), :])
    for j in range(span):
        block, at, mine = place(j)
        for t in range(4):
            part = slice(t * BLOCK, (t + 1) * BLOCK)
            rows = jnp.where(mine, own[at, part, :], other[at, part, :])
            if t < 2:
                rows = rows.astype(jnp.float32) * as_column(inverse[block, t : t + 1, :]) * gains[t]
            win[t, j * BLOCK : (j + 1) * BLOCK, :] = rows.astype(jnp.bfloat16)

    def clip_of(offset, shape, axis):
        token = lax.rem(first * BLOCK + offset + lax.broadcasted_iota(jnp.int32, shape, axis), total)
        clip = jnp.zeros(shape, jnp.int32)
        for end in ends:
            clip = clip + (token >= end).astype(jnp.int32)
        return clip, (clip == long_clip) == (core == 0)

    key_clip, key_valid = clip_of(0, (1, width), 1)
    key_clip = jnp.where(key_valid, key_clip, -1)
    keys = win[1]
    values = win[2]
    sums[...] = jnp.zeros_like(sums)
    query_total = jnp.zeros((1, HEAD_DIM), jnp.float32)

    nt = (((1,), (1,)), ((), ()))
    tn = (((0,), (0,)), ((), ()))
    ones = jnp.ones((8, HEAD_DIM), jnp.bfloat16)

    def row_sums(products):
        return sum(
            lax.dot_general(ones, part.astype(jnp.bfloat16), nt, preferred_element_type=jnp.float32)[0:1]
            for part in halves(products)
        )

    def put_sums(start, t, products):
        row = row_sums(products)
        for r in range(products.shape[0] // BLOCK):
            block = lax.rem(first + start // BLOCK + r, blocks)
            sums[block, t : t + 1, :] = row[:, r * BLOCK : (r + 1) * BLOCK]

    bounds = (0, span // 2, span)
    parts = [slice(b * BLOCK, e * BLOCK) for b, e in zip(bounds, bounds[1:])]

    def start(part):
        return lax.dot_general(win[0, part, :], keys, nt, preferred_element_type=jnp.float32)

    raw = start(parts[0])
    for i, part in enumerate(parts):
        query = win[0, part, :]
        grad = win[3, part, :].astype(jnp.float32)
        row_clip, row_valid = clip_of(part.start, (part.stop - part.start, 1), 0)
        row_clip = jnp.where(row_valid, row_clip, -2)
        scores = jnp.where(row_clip == key_clip, raw, masked_score)
        row_max = jnp.max(scores, axis=1, keepdims=True)
        if i + 1 < len(parts):
            raw = start(parts[i + 1])
        weights = jnp.exp2(scores - row_max)
        row_total = jnp.sum(weights, axis=1, keepdims=True)
        row_inv = jnp.where(row_valid, 1.0 / row_total, 0.0)
        low = weights.astype(jnp.bfloat16)
        attended = (jnp.dot(low, values, preferred_element_type=jnp.float32) * row_inv).astype(jnp.bfloat16)
        grad = grad * row_inv
        delta = jnp.sum(grad * attended.astype(jnp.float32), axis=1, keepdims=True)
        grad = grad.astype(jnp.bfloat16)
        dots = lax.dot_general(grad, values, nt, preferred_element_type=jnp.float32)
        grad_scores = (weights * (dots - delta)).astype(jnp.bfloat16)
        query_norm_grad = jnp.dot(grad_scores, keys, preferred_element_type=jnp.float32) * scale
        value_part = lax.dot_general(low, grad, tn, preferred_element_type=jnp.float32)
        key_part = lax.dot_general(grad_scores, query, tn, preferred_element_type=jnp.float32)
        if i == 0:
            vacc[...] = value_part
            kacc[...] = key_part
        else:
            vacc[...] += value_part
            kacc[...] += key_part
        products = query_norm_grad * (query.astype(jnp.float32) * (1.0 / fold))
        query_total = query_total + jnp.sum(products, axis=0, keepdims=True)
        put_sums(part.start, 0, products)
        res[0, part, :] = query_norm_grad.astype(jnp.bfloat16)
        res[2, part, :] = attended
    key_norm_grad = kacc[...] * (scale / fold)
    products = key_norm_grad * keys.astype(jnp.float32)
    key_total = jnp.sum(products, axis=0, keepdims=True)
    put_sums(0, 1, products)
    res[1] = key_norm_grad.astype(jnp.bfloat16)
    res[3] = vacc[...].astype(jnp.bfloat16)

    for j in range(blocks):
        _, at, mine = place(j)

        def store(out, at=at, j=j):
            if j >= span:
                out[at] = jnp.zeros(out.shape[1:], out.dtype)
                return
            for t in range(4):
                out[at, t * BLOCK : (t + 1) * BLOCK, :] = res[t, j * BLOCK : (j + 1) * BLOCK, :]

        pl.when(mine)(functools.partial(store, own_out))
        pl.when(jnp.logical_not(mine))(functools.partial(store, other_out))

    for block in range(blocks):
        sums[block, 2:3, :] = query_total
        sums[block, 3:4, :] = key_total


def final_kernel(
    total_width,
    queries,
    keys,
    squares,
    query_gain,
    key_gain,
    inner,
    back,
    attended,
    query_grad,
    key_grad,
    value_grad,
):
    heads = query_gain.shape[0]
    invs, factors = [], []
    lines = jnp.sum(inner[...], axis=0)
    for t, inverse in enumerate(inverses(squares, total_width)):
        invs.append(jnp.broadcast_to(inverse, (BLOCK, HEAD_DIM)))
        factor = inverse * inverse * as_column(lines[t : t + 1]) / total_width
        factors.append(jnp.broadcast_to(factor, (BLOCK, HEAD_DIM)))
    for h in range(heads):
        cols = slice(h * HEAD_DIM, (h + 1) * HEAD_DIM)
        for t, (ref, gain, grad) in enumerate(((queries, query_gain, query_grad), (keys, key_gain, key_grad))):
            norm_grad = back[h, t * BLOCK : (t + 1) * BLOCK, :].astype(jnp.float32)
            scaled = invs[t] * gain[h : h + 1, :] * norm_grad
            grad[0, :, cols] = (scaled - ref[0, :, cols].astype(jnp.float32) * factors[t]).astype(jnp.bfloat16)
        attended[0, :, cols] = back[h, 2 * BLOCK : 3 * BLOCK, :]
        value_grad[0, :, cols] = back[h, 3 * BLOCK : 4 * BLOCK, :]


def local(queries, keys, values, grad_out, lengths, query_gain, key_gain):
    rows, width = queries.shape[1:]
    heads = width // HEAD_DIM
    total_width = width * lax.axis_size("section")
    seq = lax.axis_size("seq")
    chips = seq // 2
    same_core = [[2 * z + c for z in range(chips)] for c in range(2)]
    other_core = [(i, i ^ 1) for i in range(seq)]
    query_gain, key_gain = query_gain.reshape(heads, HEAD_DIM), key_gain.reshape(heads, HEAD_DIM)
    chunk = jax.ShapeDtypeStruct((chips, 4 * rows, HEAD_DIM), jnp.bfloat16)

    def exchange(chunks):
        return lax.all_to_all(chunks, "seq", 0, 0, axis_index_groups=same_core, tiled=True)

    def swap(array):
        return lax.ppermute(array, "seq", other_core)

    hbm = pl.BlockSpec(memory_space=pl.ANY)
    packed = pl.pallas_call(
        pack_kernel,
        out_shape=chunk,
        in_specs=[hbm] * 4,
        out_specs=hbm,
        scratch_shapes=[
            pltpu.VMEM((4, 1, rows, width), jnp.bfloat16),
            pltpu.VMEM((heads, 4 * rows, HEAD_DIM), jnp.bfloat16),
            pltpu.SemaphoreType.DMA((4,)),
            pltpu.SemaphoreType.DMA((4,)),
        ],
        name="pack",
    )(queries, keys, values, grad_out)
    own = exchange(packed)
    squares = pl.pallas_call(
        squares_kernel,
        out_shape=jax.ShapeDtypeStruct((2, rows), jnp.float32),
        in_specs=[VMEM] * 2,
        out_specs=VMEM,
        name="squares",
    )(queries, keys)
    squares = lax.all_gather(squares, "section")
    inverse = lax.rsqrt(jnp.sum(squares, axis=0) / total_width + norm_eps)
    inverse = jnp.broadcast_to(inverse, (seq, 2, rows))
    own, inverse = lax.optimization_barrier((own, inverse))
    other = swap(own)
    inverse = lax.all_to_all(inverse, "seq", 0, 0, tiled=True)

    window = (chips + 1) * BLOCK
    own_out, other_out, sums = pl.pallas_call(
        functools.partial(attention_kernel, seq),
        out_shape=(chunk, chunk, jax.ShapeDtypeStruct((seq, 4, HEAD_DIM), jnp.float32)),
        in_specs=[SMEM] + [VMEM] * 5,
        out_specs=[VMEM] * 3,
        scratch_shapes=[
            pltpu.VMEM((4, window, HEAD_DIM), jnp.bfloat16),
            pltpu.VMEM((window, HEAD_DIM), jnp.float32),
            pltpu.VMEM((window, HEAD_DIM), jnp.float32),
            pltpu.VMEM((4, window, HEAD_DIM), jnp.bfloat16),
        ],
        compiler_params=pltpu.CompilerParams(vmem_limit_bytes=40 * 2**20),
        cost_estimate=pl.CostEstimate(
            flops=12 * window * window * HEAD_DIM,
            transcendentals=window * window,
            bytes_accessed=16 * chips * rows * HEAD_DIM * 2,
        ),
        name="attention",
    )(lengths, own, other, inverse, query_gain, key_gain)

    merged = own_out + swap(other_out)
    sums = lax.all_to_all(sums, "seq", 0, 0, tiled=True)
    sums, merged = lax.optimization_barrier((sums, merged))
    back = exchange(merged)
    sums = jnp.sum(sums[: 2 * heads].reshape(heads, 2, 4, HEAD_DIM), axis=1)
    inner = lax.all_gather(jnp.sum(sums[:, 0:2], axis=0), "section")
    gains = lax.psum((sums[:, 2] / query_gain, sums[:, 3] / key_gain), "dp")

    whole = jax.ShapeDtypeStruct((1, rows, width), jnp.bfloat16)
    grads = pl.pallas_call(
        functools.partial(final_kernel, total_width),
        out_shape=(whole, whole, whole, whole),
        in_specs=[VMEM] * 7,
        out_specs=[VMEM] * 4,
        compiler_params=pltpu.CompilerParams(vmem_limit_bytes=12 * 2**20),
        name="final",
    )(queries, keys, squares, query_gain, key_gain, inner, back)
    return (*grads, gains[0].reshape(width), gains[1].reshape(width))


def solution(mesh):
    rows = P("dp", "seq", "section")
    features = P("section")
    return jax.shard_map(
        local,
        mesh=mesh,
        in_specs=(rows, rows, rows, rows, P("dp", None), features, features),
        out_specs=(rows, rows, rows, rows, features, features),
        check_vma=False,
    )
```

```python
import functools
import math

import jax
import jax.numpy as jnp
from jax import lax
from jax.experimental import pallas as pl
from jax.experimental.pallas import tpu as pltpu
from jax.sharding import PartitionSpec as P

HEAD_DIM = 128
BLOCK = 128
norm_eps = 1e-06
masked_score = -1e30

VMEM = pl.BlockSpec(memory_space=pltpu.VMEM)
SMEM = pl.BlockSpec(memory_space=pltpu.SMEM)


def as_row(column):
    return jnp.broadcast_to(column, (BLOCK, BLOCK)).T[0:1]


def as_column(row):
    return jnp.broadcast_to(row, (BLOCK, BLOCK)).T[:, 0:1]


def inverses(squares, total_width):
    summed = jnp.sum(squares[...], axis=0)
    inverse = lax.rsqrt(summed / total_width + norm_eps)
    return as_column(inverse[0:1]), as_column(inverse[1:2])


def squares_kernel(queries, keys, out):
    for t, ref in enumerate((queries, keys)):
        floats = ref[0].astype(jnp.float32)
        out[t : t + 1, :] = as_row(jnp.sum(floats * floats, axis=1, keepdims=True))


def pack_kernel(queries, keys, values, grad_out, out, held, buffer, in_sems, out_sems):
    heads = buffer.shape[0]
    refs = (queries, keys, values, grad_out)
    arrive = [pltpu.make_async_copy(ref, held.at[t], in_sems.at[t]) for t, ref in enumerate(refs)]
    for copy in arrive:
        copy.start()
    leave = []
    for t in range(4):
        arrive[t].wait()
        lines = pl.ds(t * BLOCK, BLOCK)
        for h in range(heads):
            buffer[h, lines, :] = held[t, 0, :, h * HEAD_DIM : (h + 1) * HEAD_DIM]
        place = out.at[pl.ds(0, heads), lines, :]
        leave.append(pltpu.make_async_copy(buffer.at[:, lines, :], place, out_sems.at[t]))
        leave[t].start()
    for copy in leave:
        copy.wait()


def halves(floats):
    high = floats.astype(jnp.bfloat16).astype(jnp.float32)
    return [high, floats - high]


def attention_kernel(
    blocks,
    lengths,
    own,
    other,
    inverse,
    query_gain,
    key_gain,
    own_out,
    other_out,
    sums,
    win,
    kacc,
    vacc,
    res,
):
    span = win.shape[1] // BLOCK
    width = span * BLOCK
    total = blocks * BLOCK
    scale = 1.0 / math.sqrt(HEAD_DIM)
    core = lax.rem(lax.axis_index("seq"), 2)
    head = jnp.minimum(lax.div(lax.axis_index("seq"), 2), query_gain.shape[0] - 1)
    ends = [lengths[0, 0]]
    long_clip = jnp.int32(0)
    begin = jnp.int32(0)
    for c in range(1, 4):
        is_long = lengths[0, c] == total // 2
        long_clip = jnp.where(is_long, c, long_clip)
        begin = jnp.where(is_long, ends[-1], begin)
        ends.append(ends[-1] + lengths[0, c])
    first = lax.rem(lax.div(begin, BLOCK) + core * (blocks // 2), blocks)

    def place(j):
        block = lax.rem(first + j, blocks)
        return block, lax.div(block, 2), lax.rem(block, 2) == core

    fold = scale * math.log2(math.e)
    gains = (query_gain[pl.ds(head, 1), :] * fold, key_gain[pl.ds(head, 1), :])
    for j in range(span):
        block, at, mine = place(j)
        for t in range(4):
            part = slice(t * BLOCK, (t + 1) * BLOCK)
            rows = jnp.where(mine, own[at, part, :], other[at, part, :])
            if t < 2:
                rows = rows.astype(jnp.float32) * as_column(inverse[block, t : t + 1, :]) * gains[t]
            win[t, j * BLOCK : (j + 1) * BLOCK, :] = rows.astype(jnp.bfloat16)

    def clip_of(offset, shape, axis):
        token = lax.rem(first * BLOCK + offset + lax.broadcasted_iota(jnp.int32, shape, axis), total)
        clip = jnp.zeros(shape, jnp.int32)
        for end in ends:
            clip = clip + (token >= end).astype(jnp.int32)
        return clip, (clip == long_clip) == (core == 0)

    key_clip, key_valid = clip_of(0, (1, width), 1)
    key_clip = jnp.where(key_valid, key_clip, -1)
    keys = win[1]
    values = win[2]
    sums[...] = jnp.zeros_like(sums)
    query_total = jnp.zeros((1, HEAD_DIM), jnp.float32)

    nt = (((1,), (1,)), ((), ()))
    tn = (((0,), (0,)), ((), ()))
    ones = jnp.ones((8, HEAD_DIM), jnp.bfloat16)

    def row_sums(products):
        return sum(
            lax.dot_general(ones, part.astype(jnp.bfloat16), nt, preferred_element_type=jnp.float32)[0:1]
            for part in halves(products)
        )

    def put_sums(start, t, products):
        row = row_sums(products)
        for r in range(products.shape[0] // BLOCK):
            block = lax.rem(first + start // BLOCK + r, blocks)
            sums[block, t : t + 1, :] = row[:, r * BLOCK : (r + 1) * BLOCK]

    bounds = (0, span // 2, span)
    parts = [slice(b * BLOCK, e * BLOCK) for b, e in zip(bounds, bounds[1:])]

    def start(part):
        return lax.dot_general(win[0, part, :], keys, nt, preferred_element_type=jnp.float32)

    raw = start(parts[0])
    for i, part in enumerate(parts):
        query = win[0, part, :]
        grad = win[3, part, :].astype(jnp.float32)
        row_clip, row_valid = clip_of(part.start, (part.stop - part.start, 1), 0)
        row_clip = jnp.where(row_valid, row_clip, -2)
        scores = jnp.where(row_clip == key_clip, raw, masked_score)
        row_max = jnp.max(scores, axis=1, keepdims=True)
        if i + 1 < len(parts):
            raw = start(parts[i + 1])
        weights = jnp.exp2(scores - row_max)
        row_total = jnp.sum(weights, axis=1, keepdims=True)
        row_inv = jnp.where(row_valid, 1.0 / row_total, 0.0)
        low = weights.astype(jnp.bfloat16)
        attended = (jnp.dot(low, values, preferred_element_type=jnp.float32) * row_inv).astype(jnp.bfloat16)
        grad = grad * row_inv
        delta = jnp.sum(grad * attended.astype(jnp.float32), axis=1, keepdims=True)
        grad = grad.astype(jnp.bfloat16)
        dots = lax.dot_general(grad, values, nt, preferred_element_type=jnp.float32)
        grad_scores = (weights * (dots - delta)).astype(jnp.bfloat16)
        query_norm_grad = jnp.dot(grad_scores, keys, preferred_element_type=jnp.float32) * scale
        value_part = lax.dot_general(low, grad, tn, preferred_element_type=jnp.float32)
        key_part = lax.dot_general(grad_scores, query, tn, preferred_element_type=jnp.float32)
        if i == 0:
            vacc[...] = value_part
            kacc[...] = key_part
        else:
            vacc[...] += value_part
            kacc[...] += key_part
        products = query_norm_grad * (query.astype(jnp.float32) * (1.0 / fold))
        query_total = query_total + jnp.sum(products, axis=0, keepdims=True)
        put_sums(part.start, 0, products)
        res[0, part, :] = query_norm_grad.astype(jnp.bfloat16)
        res[2, part, :] = attended
    key_norm_grad = kacc[...] * (scale / fold)
    products = key_norm_grad * keys.astype(jnp.float32)
    key_total = jnp.sum(products, axis=0, keepdims=True)
    put_sums(0, 1, products)
    res[1] = key_norm_grad.astype(jnp.bfloat16)
    res[3] = vacc[...].astype(jnp.bfloat16)

    for j in range(blocks):
        _, at, mine = place(j)

        def store(out, at=at, j=j):
            if j >= span:
                out[at] = jnp.zeros(out.shape[1:], out.dtype)
                return
            for t in range(4):
                out[at, t * BLOCK : (t + 1) * BLOCK, :] = res[t, j * BLOCK : (j + 1) * BLOCK, :]

        pl.when(mine)(functools.partial(store, own_out))
        pl.when(jnp.logical_not(mine))(functools.partial(store, other_out))

    for block in range(blocks):
        sums[block, 2:3, :] = query_total
        sums[block, 3:4, :] = key_total


def final_kernel(
    total_width,
    queries,
    keys,
    squares,
    query_gain,
    key_gain,
    inner,
    back,
    attended,
    query_grad,
    key_grad,
    value_grad,
):
    heads = query_gain.shape[0]
    invs, factors = [], []
    lines = jnp.sum(inner[...], axis=0)
    for t, inverse in enumerate(inverses(squares, total_width)):
        invs.append(jnp.broadcast_to(inverse, (BLOCK, HEAD_DIM)))
        factor = inverse * inverse * as_column(lines[t : t + 1]) / total_width
        factors.append(jnp.broadcast_to(factor, (BLOCK, HEAD_DIM)))
    for h in range(heads):
        cols = slice(h * HEAD_DIM, (h + 1) * HEAD_DIM)
        for t, (ref, gain, grad) in enumerate(((queries, query_gain, query_grad), (keys, key_gain, key_grad))):
            norm_grad = back[h, t * BLOCK : (t + 1) * BLOCK, :].astype(jnp.float32)
            scaled = invs[t] * gain[h : h + 1, :] * norm_grad
            grad[0, :, cols] = (scaled - ref[0, :, cols].astype(jnp.float32) * factors[t]).astype(jnp.bfloat16)
        attended[0, :, cols] = back[h, 2 * BLOCK : 3 * BLOCK, :]
        value_grad[0, :, cols] = back[h, 3 * BLOCK : 4 * BLOCK, :]


def local(queries, keys, values, grad_out, lengths, query_gain, key_gain):
    rows, width = queries.shape[1:]
    heads = width // HEAD_DIM
    total_width = width * lax.axis_size("section")
    seq = lax.axis_size("seq")
    chips = seq // 2
    same_core = [[2 * z + c for z in range(chips)] for c in range(2)]
    other_core = [(i, i ^ 1) for i in range(seq)]
    query_gain, key_gain = query_gain.reshape(heads, HEAD_DIM), key_gain.reshape(heads, HEAD_DIM)
    chunk = jax.ShapeDtypeStruct((chips, 4 * rows, HEAD_DIM), jnp.bfloat16)

    def exchange(chunks):
        return lax.all_to_all(chunks, "seq", 0, 0, axis_index_groups=same_core, tiled=True)

    def swap(array):
        return lax.ppermute(array, "seq", other_core)

    hbm = pl.BlockSpec(memory_space=pl.ANY)
    packed = pl.pallas_call(
        pack_kernel,
        out_shape=chunk,
        in_specs=[hbm] * 4,
        out_specs=hbm,
        scratch_shapes=[
            pltpu.VMEM((4, 1, rows, width), jnp.bfloat16),
            pltpu.VMEM((heads, 4 * rows, HEAD_DIM), jnp.bfloat16),
            pltpu.SemaphoreType.DMA((4,)),
            pltpu.SemaphoreType.DMA((4,)),
        ],
        name="pack",
    )(queries, keys, values, grad_out)
    own = exchange(packed)
    squares = pl.pallas_call(
        squares_kernel,
        out_shape=jax.ShapeDtypeStruct((2, rows), jnp.float32),
        in_specs=[VMEM] * 2,
        out_specs=VMEM,
        name="squares",
    )(queries, keys)
    squares = lax.all_gather(squares, "section")
    inverse = lax.rsqrt(jnp.sum(squares, axis=0) / total_width + norm_eps)
    inverse = jnp.broadcast_to(inverse, (seq, 2, rows))
    own, inverse, lengths = lax.optimization_barrier((own, inverse, jnp.maximum(lengths, 0)))
    other = swap(own)
    inverse = lax.all_to_all(inverse, "seq", 0, 0, tiled=True)

    window = (chips + 1) * BLOCK
    own_out, other_out, sums = pl.pallas_call(
        functools.partial(attention_kernel, seq),
        out_shape=(chunk, chunk, jax.ShapeDtypeStruct((seq, 4, HEAD_DIM), jnp.float32)),
        in_specs=[SMEM] + [VMEM] * 5,
        out_specs=[VMEM] * 3,
        scratch_shapes=[
            pltpu.VMEM((4, window, HEAD_DIM), jnp.bfloat16),
            pltpu.VMEM((window, HEAD_DIM), jnp.float32),
            pltpu.VMEM((window, HEAD_DIM), jnp.float32),
            pltpu.VMEM((4, window, HEAD_DIM), jnp.bfloat16),
        ],
        compiler_params=pltpu.CompilerParams(vmem_limit_bytes=40 * 2**20),
        cost_estimate=pl.CostEstimate(
            flops=12 * window * window * HEAD_DIM,
            transcendentals=window * window,
            bytes_accessed=16 * chips * rows * HEAD_DIM * 2,
        ),
        name="attention",
    )(lengths, own, other, inverse, query_gain, key_gain)

    merged = own_out + swap(other_out)
    sums = lax.all_to_all(sums, "seq", 0, 0, tiled=True)
    sums, merged = lax.optimization_barrier((sums, merged))
    back = exchange(merged)
    sums = jnp.sum(sums[: 2 * heads].reshape(heads, 2, 4, HEAD_DIM), axis=1)
    inner = lax.all_gather(jnp.sum(sums[:, 0:2], axis=0), "section")
    gains = lax.psum((sums[:, 2] / query_gain, sums[:, 3] / key_gain), "dp")

    whole = jax.ShapeDtypeStruct((1, rows, width), jnp.bfloat16)
    grads = pl.pallas_call(
        functools.partial(final_kernel, total_width),
        out_shape=(whole, whole, whole, whole),
        in_specs=[VMEM] * 7,
        out_specs=[VMEM] * 4,
        compiler_params=pltpu.CompilerParams(vmem_limit_bytes=12 * 2**20),
        name="final",
    )(queries, keys, squares, query_gain, key_gain, inner, back)
    return (*grads, gains[0].reshape(width), gains[1].reshape(width))


def solution(mesh):
    rows = P("dp", "seq", "section")
    features = P("section")
    return jax.shard_map(
        local,
        mesh=mesh,
        in_specs=(rows, rows, rows, rows, P("dp", None), features, features),
        out_specs=(rows, rows, rows, rows, features, features),
        check_vma=False,
    )
```

```python
import functools
import math

import jax
import jax.numpy as jnp
from jax import lax
from jax.experimental import pallas as pl
from jax.experimental.pallas import tpu as pltpu
from jax.sharding import PartitionSpec as P

HEAD_DIM = 128
BLOCK = 128
norm_eps = 1e-06
masked_score = -1e30

VMEM = pl.BlockSpec(memory_space=pltpu.VMEM)
SMEM = pl.BlockSpec(memory_space=pltpu.SMEM)


def as_row(column):
    return jnp.broadcast_to(column, (BLOCK, BLOCK)).T[0:1]


def as_column(row):
    return jnp.broadcast_to(row, (BLOCK, BLOCK)).T[:, 0:1]


def inverses(squares, total_width):
    summed = jnp.sum(squares[...], axis=0)
    inverse = lax.rsqrt(summed / total_width + norm_eps)
    return as_column(inverse[0:1]), as_column(inverse[1:2])


def squares_kernel(queries, keys, out):
    for t, ref in enumerate((queries, keys)):
        floats = ref[0].astype(jnp.float32)
        out[t : t + 1, :] = as_row(jnp.sum(floats * floats, axis=1, keepdims=True))


def pack_kernel(queries, keys, values, grad_out, out, held, buffer, in_sems, out_sems):
    heads = buffer.shape[0]
    refs = (queries, keys, values, grad_out)
    arrive = [pltpu.make_async_copy(ref, held.at[t], in_sems.at[t]) for t, ref in enumerate(refs)]
    for copy in arrive:
        copy.start()
    leave = []
    for t in range(4):
        arrive[t].wait()
        lines = pl.ds(t * BLOCK, BLOCK)
        for h in range(heads):
            buffer[h, lines, :] = held[t, 0, :, h * HEAD_DIM : (h + 1) * HEAD_DIM]
        place = out.at[pl.ds(0, heads), lines, :]
        leave.append(pltpu.make_async_copy(buffer.at[:, lines, :], place, out_sems.at[t]))
        leave[t].start()
    for copy in leave:
        copy.wait()


def halves(floats):
    high = floats.astype(jnp.bfloat16).astype(jnp.float32)
    return [high, floats - high]


def attention_kernel(
    blocks,
    lengths,
    own,
    other,
    inverse,
    query_gain,
    key_gain,
    own_out,
    other_out,
    sums,
    win,
    kacc,
    vacc,
    res,
):
    span = win.shape[1] // BLOCK
    width = span * BLOCK
    total = blocks * BLOCK
    scale = 1.0 / math.sqrt(HEAD_DIM)
    core = lax.rem(lax.axis_index("seq"), 2)
    head = jnp.minimum(lax.div(lax.axis_index("seq"), 2), query_gain.shape[0] - 1)
    ends = [lengths[0, 0]]
    long_clip = jnp.int32(0)
    begin = jnp.int32(0)
    for c in range(1, 4):
        is_long = lengths[0, c] == total // 2
        long_clip = jnp.where(is_long, c, long_clip)
        begin = jnp.where(is_long, ends[-1], begin)
        ends.append(ends[-1] + lengths[0, c])
    first = lax.rem(lax.div(begin, BLOCK) + core * (blocks // 2), blocks)

    def place(j):
        block = lax.rem(first + j, blocks)
        return block, lax.div(block, 2), lax.rem(block, 2) == core

    fold = scale * math.log2(math.e)
    gains = (query_gain[pl.ds(head, 1), :] * fold, key_gain[pl.ds(head, 1), :])
    for j in range(span):
        block, at, mine = place(j)
        for t in range(4):
            part = slice(t * BLOCK, (t + 1) * BLOCK)
            rows = jnp.where(mine, own[at, part, :], other[at, part, :])
            if t < 2:
                rows = rows.astype(jnp.float32) * as_column(inverse[block, t : t + 1, :]) * gains[t]
            win[t, j * BLOCK : (j + 1) * BLOCK, :] = rows.astype(jnp.bfloat16)

    def clip_of(offset, shape, axis):
        token = lax.rem(first * BLOCK + offset + lax.broadcasted_iota(jnp.int32, shape, axis), total)
        clip = jnp.zeros(shape, jnp.int32)
        for end in ends:
            clip = clip + (token >= end).astype(jnp.int32)
        return clip, (clip == long_clip) == (core == 0)

    key_clip, key_valid = clip_of(0, (1, width), 1)
    key_clip = jnp.where(key_valid, key_clip, -1)
    keys = win[1]
    values = win[2]
    sums[...] = jnp.zeros_like(sums)
    query_total = jnp.zeros((1, HEAD_DIM), jnp.float32)

    nt = (((1,), (1,)), ((), ()))
    tn = (((0,), (0,)), ((), ()))
    ones = jnp.ones((8, HEAD_DIM), jnp.bfloat16)

    def row_sums(products):
        return sum(
            lax.dot_general(ones, part.astype(jnp.bfloat16), nt, preferred_element_type=jnp.float32)[0:1]
            for part in halves(products)
        )

    def put_sums(start, t, products):
        row = row_sums(products)
        for r in range(products.shape[0] // BLOCK):
            block = lax.rem(first + start // BLOCK + r, blocks)
            sums[block, t : t + 1, :] = row[:, r * BLOCK : (r + 1) * BLOCK]

    bounds = (0, span // 2, span)
    parts = [slice(b * BLOCK, e * BLOCK) for b, e in zip(bounds, bounds[1:])]

    def start(part):
        return lax.dot_general(win[0, part, :], keys, nt, preferred_element_type=jnp.float32)

    raw = start(parts[0])
    for i, part in enumerate(parts):
        query = win[0, part, :]
        grad = win[3, part, :].astype(jnp.float32)
        row_clip, row_valid = clip_of(part.start, (part.stop - part.start, 1), 0)
        row_clip = jnp.where(row_valid, row_clip, -2)
        scores = jnp.where(row_clip == key_clip, raw, masked_score)
        row_max = jnp.max(scores, axis=1, keepdims=True)
        if i + 1 < len(parts):
            raw = start(parts[i + 1])
        weights = jnp.exp2(scores - row_max)
        row_total = jnp.sum(weights, axis=1, keepdims=True)
        row_inv = jnp.where(row_valid, 1.0 / row_total, 0.0)
        low = weights.astype(jnp.bfloat16)
        attended = (jnp.dot(low, values, preferred_element_type=jnp.float32) * row_inv).astype(jnp.bfloat16)
        grad = grad * row_inv
        delta = jnp.sum(grad * attended.astype(jnp.float32), axis=1, keepdims=True)
        grad = grad.astype(jnp.bfloat16)
        dots = lax.dot_general(grad, values, nt, preferred_element_type=jnp.float32)
        grad_scores = (weights * (dots - delta)).astype(jnp.bfloat16)
        query_norm_grad = jnp.dot(grad_scores, keys, preferred_element_type=jnp.float32) * scale
        value_part = lax.dot_general(low, grad, tn, preferred_element_type=jnp.float32)
        key_part = lax.dot_general(grad_scores, query, tn, preferred_element_type=jnp.float32)
        if i == 0:
            vacc[...] = value_part
            kacc[...] = key_part
        else:
            vacc[...] += value_part
            kacc[...] += key_part
        products = query_norm_grad * (query.astype(jnp.float32) * (1.0 / fold))
        query_total = query_total + jnp.sum(products, axis=0, keepdims=True)
        put_sums(part.start, 0, products)
        res[0, part, :] = query_norm_grad.astype(jnp.bfloat16)
        res[2, part, :] = attended
    key_norm_grad = kacc[...] * (scale / fold)
    products = key_norm_grad * keys.astype(jnp.float32)
    key_total = jnp.sum(products, axis=0, keepdims=True)
    put_sums(0, 1, products)
    res[1] = key_norm_grad.astype(jnp.bfloat16)
    res[3] = vacc[...].astype(jnp.bfloat16)

    for j in range(blocks):
        _, at, mine = place(j)

        def store(out, at=at, j=j):
            if j >= span:
                out[at] = jnp.zeros(out.shape[1:], out.dtype)
                return
            for t in range(4):
                out[at, t * BLOCK : (t + 1) * BLOCK, :] = res[t, j * BLOCK : (j + 1) * BLOCK, :]

        pl.when(mine)(functools.partial(store, own_out))
        pl.when(jnp.logical_not(mine))(functools.partial(store, other_out))

    for block in range(blocks):
        sums[block, 2:3, :] = query_total
        sums[block, 3:4, :] = key_total


def final_kernel(
    total_width,
    queries,
    keys,
    squares,
    query_gain,
    key_gain,
    inner,
    back,
    attended,
    query_grad,
    key_grad,
    value_grad,
):
    heads = query_gain.shape[0]
    invs, factors = [], []
    lines = jnp.sum(inner[...], axis=0)
    for t, inverse in enumerate(inverses(squares, total_width)):
        invs.append(jnp.broadcast_to(inverse, (BLOCK, HEAD_DIM)))
        factor = inverse * inverse * as_column(lines[t : t + 1]) / total_width
        factors.append(jnp.broadcast_to(factor, (BLOCK, HEAD_DIM)))
    for h in range(heads):
        cols = slice(h * HEAD_DIM, (h + 1) * HEAD_DIM)
        for t, (ref, gain, grad) in enumerate(((queries, query_gain, query_grad), (keys, key_gain, key_grad))):
            norm_grad = back[h, t * BLOCK : (t + 1) * BLOCK, :].astype(jnp.float32)
            scaled = invs[t] * gain[h : h + 1, :] * norm_grad
            grad[0, :, cols] = (scaled - ref[0, :, cols].astype(jnp.float32) * factors[t]).astype(jnp.bfloat16)
        attended[0, :, cols] = back[h, 2 * BLOCK : 3 * BLOCK, :]
        value_grad[0, :, cols] = back[h, 3 * BLOCK : 4 * BLOCK, :]


def local(queries, keys, values, grad_out, lengths, query_gain, key_gain):
    rows, width = queries.shape[1:]
    heads = width // HEAD_DIM
    total_width = width * lax.axis_size("section")
    seq = lax.axis_size("seq")
    chips = seq // 2
    same_core = [[2 * z + c for z in range(chips)] for c in range(2)]
    other_core = [(i, i ^ 1) for i in range(seq)]
    query_gain, key_gain = query_gain.reshape(heads, HEAD_DIM), key_gain.reshape(heads, HEAD_DIM)
    chunk = jax.ShapeDtypeStruct((chips, 4 * rows, HEAD_DIM), jnp.bfloat16)

    def exchange(chunks):
        return lax.all_to_all(chunks, "seq", 0, 0, axis_index_groups=same_core, tiled=True)

    def swap(array):
        return lax.ppermute(array, "seq", other_core)

    hbm = pl.BlockSpec(memory_space=pl.ANY)
    packed = pl.pallas_call(
        pack_kernel,
        out_shape=chunk,
        in_specs=[hbm] * 4,
        out_specs=hbm,
        scratch_shapes=[
            pltpu.VMEM((4, 1, rows, width), jnp.bfloat16),
            pltpu.VMEM((heads, 4 * rows, HEAD_DIM), jnp.bfloat16),
            pltpu.SemaphoreType.DMA((4,)),
            pltpu.SemaphoreType.DMA((4,)),
        ],
        name="pack",
    )(queries, keys, values, grad_out)
    own = exchange(packed)
    squares = pl.pallas_call(
        squares_kernel,
        out_shape=jax.ShapeDtypeStruct((2, rows), jnp.float32),
        in_specs=[VMEM] * 2,
        out_specs=VMEM,
        name="squares",
    )(queries, keys)
    squares = lax.all_gather(squares, "section")
    inverse = lax.rsqrt(jnp.sum(squares, axis=0) / total_width + norm_eps)
    inverse = jnp.broadcast_to(inverse, (seq, 2, rows))
    own, inverse, lengths = lax.optimization_barrier((own, inverse, jnp.maximum(lengths, 0)))
    other = swap(own)
    inverse = lax.all_to_all(inverse, "seq", 0, 0, tiled=True)

    window = (chips + 1) * BLOCK
    own_out, other_out, sums = pl.pallas_call(
        functools.partial(attention_kernel, seq),
        out_shape=(chunk, chunk, jax.ShapeDtypeStruct((seq, 4, HEAD_DIM), jnp.float32)),
        in_specs=[SMEM] + [VMEM] * 5,
        out_specs=[VMEM] * 3,
        scratch_shapes=[
            pltpu.VMEM((4, window, HEAD_DIM), jnp.bfloat16),
            pltpu.VMEM((window, HEAD_DIM), jnp.float32),
            pltpu.VMEM((window, HEAD_DIM), jnp.float32),
            pltpu.VMEM((4, window, HEAD_DIM), jnp.bfloat16),
        ],
        compiler_params=pltpu.CompilerParams(vmem_limit_bytes=40 * 2**20),
        cost_estimate=pl.CostEstimate(
            flops=12 * window * window * HEAD_DIM,
            transcendentals=window * window,
            bytes_accessed=16 * chips * rows * HEAD_DIM * 2,
        ),
        name="attention",
    )(lengths, own, other, inverse, query_gain, key_gain)

    merged = own_out + swap(other_out)
    sums = lax.all_to_all(sums, "seq", 0, 0, tiled=True)
    sums, merged = lax.optimization_barrier((sums, merged))
    back = exchange(merged)
    sums = jnp.sum(sums[: 2 * heads].reshape(heads, 2, 4, HEAD_DIM), axis=1)
    inner = lax.all_gather(jnp.sum(sums[:, 0:2], axis=0), "section")
    gains = lax.psum(jnp.concatenate([sums[:, 2] / query_gain, sums[:, 3] / key_gain]), "dp")

    whole = jax.ShapeDtypeStruct((1, rows, width), jnp.bfloat16)
    grads = pl.pallas_call(
        functools.partial(final_kernel, total_width),
        out_shape=(whole, whole, whole, whole),
        in_specs=[VMEM] * 7,
        out_specs=[VMEM] * 4,
        compiler_params=pltpu.CompilerParams(vmem_limit_bytes=12 * 2**20),
        name="final",
    )(queries, keys, squares, query_gain, key_gain, inner, back)
    return (*grads, gains[:heads].reshape(width), gains[heads:].reshape(width))


def solution(mesh):
    rows = P("dp", "seq", "section")
    features = P("section")
    return jax.shard_map(
        local,
        mesh=mesh,
        in_specs=(rows, rows, rows, rows, P("dp", None), features, features),
        out_specs=(rows, rows, rows, rows, features, features),
        check_vma=False,
    )
```
